256 devices in a mesh: dp: 2 (over core), context: 32 (over y, z), tensor: 4 (over x).
Axes of the slice: x: 4, y: 4, z: 8, core: 2. Of those that a mesh axis runs over, the one named last changes fastest.
Arguments:
- mixer_input: bfloat16 [16384, 5120], P(('dp', 'context'), 'tensor'), parts along dimension 0, may hold values from -6 to 6
- gate_z: bfloat16 [16384, 4096], P(('dp', 'context'), 'tensor'), parts along dimension 0, may hold values from -6 to 6
- dt_raw: float32 [16384, 64], P(('dp', 'context'), 'tensor'), parts along dimension 0, may hold values from -6 to 6
- dt_bias: float32 [64], P('tensor'), may hold values from -3 to 3
- a_log: float32 [64], P('tensor'), may hold values from -11 to -2.5
- d_skip: float32 [64], P('tensor'), may hold values from 0.5 to 1.5
- conv_weight: float32 [4, 5120], P(None, 'tensor'), may hold values from -3 to 3
- conv_bias: float32 [5120], P('tensor'), may hold values from -2 to 2
- norm_gain: float32 [4096], P('tensor'), may hold values from 0.25 to 1.75
- w_out: bfloat16 [4096, 4096], P('tensor'), may hold values from -0.09375 to 0.09375
- residual: bfloat16 [16384, 4096], P(('dp', 'context'), 'tensor'), parts along dimension 0, may hold values from -6 to 6
- attn_gain: float32 [4096], replicated, may hold values from 0.1 to 1.9
- w_query: bfloat16 [4096, 2048], P('context', 'tensor'), may hold values from -4 to 4
- w_key: bfloat16 [4096, 512], P('context', 'tensor'), may hold values from -4 to 4
- value_weight: bfloat16 [4096, 512], P('context', 'tensor'), may hold values from -0.09375 to 0.09375
- doc_ids: int32 [16384], P(('dp', 'context')), parts along dimension 0, may hold values from 0 to 15, never falling along the last dimension, each value on 1 to 4352 neighbouring positions
- owners: int32 [64, 32], P(('dp', 'context')), parts along dimension 0, may hold values from 0 to 31, each once within a row
Outputs:
- hidden_out: bfloat16 [16384, 4096], P(('dp', 'context'), 'tensor'), parts along dimension 0
- attended: bfloat16 [16384, 2048], P(('dp', 'context'), 'tensor'), parts along dimension 0
The draws below stay inside these ranges and needn't reach their ends.
There are 2 independent parts, one for each index of `dp`. The reference program is written for one: setup_inputs(seed, part) draws one part's arguments, and reference() takes and returns one part's arrays. A program takes and returns all parts, laid end to end along the dimension named above; an argument that names none is the same for every part. Nothing has to cross between parts.
Inputs may be any that keep to these rules, and one draw needn't show every extreme that they name: `doc_ids`: ids never fall along the sequence; each document has 1 to 4352 tokens and one has exactly 4352. `owners`: row i names, for each of the 32 blocks of 8 tokens of context index i, the context index that owns it; each row is a permutation.
All inputs are finite; a program needn't handle non-finite values.
Results may differ from the reference program's by a relative error of at most 0.04.
The reference program's roundings to bfloat16 on the way (of `conv_out`, `normed_ssm`, `normed`, `values`, `probs` and `context`) count: a program that leaves them out, or rounds other values in their place, can miss the bound.
Values may be sent and summed in bfloat16 or wider, within the bound.
A program may use at most 128 MiB of HBM per device.

```python
import math
import jax
import jax.numpy as jnp
import numpy as np
from jax import lax

MODEL_DIMENSION = 4096
NH = 64
P_SIZE = 64
NS = 128
G = 4
KCONV = 4
QUERY_HEADS = 16
KEY_VALUE_HEADS = 4
HEAD_DIMENSION = 128
TOK_DEV = 256
INNER = 4096
XBC = 5120
TOKENS = 8192
QBLK = 8
DOC_MOST = 4352
N_CONTEXT = 32


def draw_a_log(key, part):
    offset_draw = jax.random.uniform(jax.random.fold_in(key, 31), (NH,), jnp.float32)
    picker = jax.random.uniform(jax.random.fold_in(key, 37), (NH,), jnp.float32)
    share_slow = 0.5
    slow_rate = jnp.log(0.5 / (0.7 * TOKENS)) + offset_draw - 0.5
    fast_rate = jnp.log(1.0 / 28.0) + offset_draw - 0.5
    return jnp.where(picker < share_slow, slow_rate, fast_rate).astype(jnp.float32)


def query_offset(key):
    random_noise = jax.random.normal(jax.random.fold_in(key, 101), (MODEL_DIMENSION, QUERY_HEADS * HEAD_DIMENSION), jnp.float32)
    return jnp.clip(random_noise, -4.0, 4.0) / math.sqrt(MODEL_DIMENSION)


def draw_w_query(key, part):
    base_rows = query_offset(key)
    return base_rows.astype(jnp.bfloat16)


def draw_w_key(key, part):
    random_noise = jax.random.normal(jax.random.fold_in(key, 107), (MODEL_DIMENSION, KEY_VALUE_HEADS * HEAD_DIMENSION), jnp.float32)
    return (jnp.clip(random_noise, -4.0, 4.0) / math.sqrt(MODEL_DIMENSION)).astype(jnp.bfloat16)


def block_levels(rng, shape, cuts, smallest, largest):
    gain, own = 1.0, jax.random.fold_in(rng, 6)
    for axis_at, blocks in cuts:
        draws = jnp.exp(jax.random.uniform(jax.random.fold_in(own, axis_at), (blocks,), jnp.float32, smallest / len(cuts), largest / len(cuts)))
        gain = gain * jnp.repeat(draws, shape[axis_at] // blocks).reshape([-1 if axis == axis_at else 1 for axis in range(len(shape))])
    return gain


def profile(count, total, most, slope):
    portions = [(1 << 20) // math.isqrt(rank ** slope) + 1 for rank in range(2, count + 1)]
    surplus, holding = total - most - (count - 1), [1] * (count - 1)
    while surplus > 0:
        movable = [i for i in range(count - 1) if holding[i] < most]
        whole, remaining = sum([portions[i] for i in movable]), surplus
        for i in movable:
            more = min(most - holding[i], max(1, remaining * portions[i] // whole), surplus)
            holding[i] = holding[i] + more
            surplus = surplus - more
    return np.array([most] + holding)


def ragged(key, amount, total, reach, slope):
    if amount == 2:
        one = jax.random.randint(key, (), max(1, total - reach), min(reach, total - 1) + 1)
        return jnp.stack([one, total - one])
    sizes = jnp.asarray(profile(amount, total, reach, slope), jnp.int32)
    pairs = (amount - 1) // 2
    donor, sink = sizes[1:1 + 2 * pairs:2], sizes[2:2 + 2 * pairs:2]
    margin = jnp.minimum(donor - 1, reach - sink)
    shifted = jax.random.randint(jax.random.fold_in(key, 1), (pairs,), 0, 1 << 20) % (margin + 1)
    sizes = sizes.at[1:1 + 2 * pairs:2].set(donor - shifted).at[2:2 + 2 * pairs:2].set(sink + shifted)
    return sizes[jax.random.permutation(jax.random.fold_in(key, 2), amount)]


def normal_values(stream_key, dims, deviation, reach, split=(), kind=jnp.bfloat16):
    values = jax.random.normal(stream_key, dims, jnp.float32) * deviation
    if len(split) > 0:
        values = block_levels(stream_key, dims, split, -0.22, 0.18) * values
    return jnp.clip(values, min=-reach, max=reach).astype(kind)


def setup_inputs(seed: int = 0, part: int = 0) -> dict:
    seeds = jax.random.split(jax.random.key(seed), 18)
    part_keys = jax.random.split(jax.random.fold_in(seeds[17], part), 18)
    return {
        "mixer_input": normal_values(part_keys[0], (TOKENS, XBC), 1.0, 6.0, ((0, 32), (1, 4))),
        "gate_z": normal_values(part_keys[1], (TOKENS, INNER), 1.0, 6.0, ((0, 32), (1, 4))),
        "dt_raw": normal_values(part_keys[2], (TOKENS, NH), 1.0, 6.0, ((0, 32), (1, 4)), jnp.float32),
        "dt_bias": normal_values(seeds[3], (NH,), 0.5, 3.0, ((0, 4),), jnp.float32),
        "a_log": draw_a_log(jax.random.fold_in(seeds[17], 71), part),
        "d_skip": jnp.clip(0.5 + 1.0 * jax.random.uniform(seeds[5], (NH,), jnp.float32) ** block_levels(seeds[5], (NH,), ((0, 4),), -0.2, 0.2), 0.5, 1.5),
        "conv_weight": normal_values(seeds[6], (KCONV, XBC), 0.5, 3.0, ((1, 4),), jnp.float32),
        "conv_bias": normal_values(seeds[7], (XBC,), 0.3, 2.0, ((0, 4),), jnp.float32),
        "norm_gain": jnp.clip(1.0 + 0.15 * jax.random.normal(seeds[8], (INNER,), jnp.float32), 0.25, 1.75),
        "w_out": normal_values(seeds[9], (INNER, MODEL_DIMENSION), INNER ** -0.5, 0.09375, ((0, 4),)),
        "residual": normal_values(part_keys[10], (TOKENS, MODEL_DIMENSION), 1.0, 6.0, ((0, 32), (1, 4))),
        "attn_gain": jnp.clip(1.0 + 0.18 * jax.random.normal(seeds[11], (MODEL_DIMENSION,), jnp.float32), 0.1, 1.9),
        "w_query": draw_w_query(jax.random.fold_in(seeds[17], 71), part),
        "w_key": draw_w_key(jax.random.fold_in(seeds[17], 71), part),
        "value_weight": normal_values(seeds[14], (MODEL_DIMENSION, KEY_VALUE_HEADS * HEAD_DIMENSION), MODEL_DIMENSION ** -0.5, 0.09375, ((0, 32), (1, 4))),
        "doc_ids": jnp.searchsorted(jnp.cumsum(ragged(part_keys[15], 16, TOKENS, DOC_MOST, 2)), jnp.arange(TOKENS), side="right").astype(jnp.int32),
        "owners": jax.vmap(lambda own: jax.random.permutation(own, N_CONTEXT))(jax.random.split(part_keys[16], N_CONTEXT)).reshape((N_CONTEXT, N_CONTEXT)).astype(jnp.int32),
    }


epsilon = 1e-05
rope_base = 500000.0

def rotate(value_matrix, positions):
    heads = value_matrix.shape[1] // HEAD_DIMENSION
    shaped = value_matrix.reshape(value_matrix.shape[0], heads, HEAD_DIMENSION)
    half_width = HEAD_DIMENSION // 2
    freqs = jnp.exp(jnp.arange(half_width, dtype=jnp.float32) * (-2.0 * math.log(rope_base) / HEAD_DIMENSION))
    angles = positions.astype(jnp.float32)[:, None] * freqs[None, :]
    cosine = jnp.cos(angles)[:, None, :]
    sine = jnp.sin(angles)[:, None, :]
    first_half = shaped[:, :, :half_width]
    second_half = shaped[:, :, half_width:]
    rotated = jnp.concatenate([first_half * cosine - second_half * sine, second_half * cosine + first_half * sine], axis=-1)
    return rotated.reshape(value_matrix.shape)

def convolve(mixer_input, conv_weight, conv_bias, doc_ids):
    value_matrix = mixer_input.astype(jnp.float32)
    lag = KCONV - 1
    padded = jnp.pad(value_matrix, ((lag, 0), (0, 0)))
    padded_docs = jnp.concatenate([jnp.full((lag,), -1, jnp.int32), doc_ids])
    running = jnp.broadcast_to(conv_bias, value_matrix.shape)
    for offset in range(KCONV):
        rows_here = padded[offset:offset + TOKENS]
        same_doc = padded_docs[offset:offset + TOKENS] == doc_ids
        running = running + conv_weight[offset] * jnp.where(same_doc[:, None], rows_here, 0.0)
    return jax.nn.silu(running).astype(jnp.bfloat16)

def state_block(conv_block, step_block, docs_block, prev_doc, a_log):
    rows_count, heads = step_block.shape
    groups = (conv_block.shape[1] - heads * P_SIZE) // (2 * NS)
    per_group = heads // groups
    shaped = conv_block.astype(jnp.float32).reshape(rows_count, groups, per_group * P_SIZE + 2 * NS)
    inputs_x = shaped[:, :, :per_group * P_SIZE].reshape(rows_count, heads, P_SIZE)
    in_b = jnp.repeat(shaped[:, :, per_group * P_SIZE:per_group * P_SIZE + NS], per_group, axis=1)
    out_c = jnp.repeat(shaped[:, :, per_group * P_SIZE + NS:], per_group, axis=1)
    cumul = jnp.cumsum(-step_block * jnp.exp(a_log), axis=0)
    row_ids = jnp.arange(rows_count, dtype=jnp.int32)
    allowed = (docs_block[:, None] == docs_block[None, :]) & (row_ids[:, None] >= row_ids[None, :])
    intersection = jnp.einsum('thn,shn->hts', out_c, in_b, precision=lax.Precision.HIGHEST)
    decays = jnp.exp(jnp.where(allowed[None], cumul.T[:, :, None] - cumul.T[:, None, :], -jnp.inf))
    weights = decays * intersection * step_block.T[:, None, :]
    outputs = jnp.einsum('hts,shp->thp', weights, inputs_x, precision=lax.Precision.HIGHEST)
    end_weight = jnp.exp(cumul[-1][None, :] - cumul) * (docs_block == docs_block[-1]).astype(jnp.float32)[:, None] * step_block
    state = jnp.einsum('sh,shp,shn->hpn', end_weight, inputs_x, in_b, precision=lax.Precision.HIGHEST)
    through = jnp.exp(cumul[-1]) * (docs_block[-1] == prev_doc).astype(jnp.float32)
    return (outputs, through, state, cumul, out_c, inputs_x)

def reference(mixer_input, gate_z, dt_raw, dt_bias, a_log, d_skip, conv_weight, conv_bias, norm_gain, w_out, residual, attn_gain, w_query, w_key, value_weight, doc_ids, owners):
    conv_out = convolve(mixer_input, conv_weight, conv_bias, doc_ids)
    step_size = jax.nn.softplus(dt_raw + dt_bias)
    blocks_conv = conv_out.reshape(N_CONTEXT, TOK_DEV, XBC)
    blocks_step = step_size.reshape(N_CONTEXT, TOK_DEV, NH)
    blocks_doc = doc_ids.reshape(N_CONTEXT, TOK_DEV)

    def advance(carried, block):
        incoming, prev_doc = carried
        conv_block, step_block, docs_block = block
        outputs, through, state, cumul, out_c, inputs_x = state_block(conv_block, step_block, docs_block, prev_doc, a_log)
        carry_on = (docs_block == prev_doc).astype(jnp.float32)
        outputs = outputs + jnp.exp(cumul)[:, :, None] * carry_on[:, None, None] * jnp.einsum('thn,hpn->thp', out_c, incoming, precision=lax.Precision.HIGHEST)
        outputs = outputs + d_skip[None, :, None] * inputs_x
        return ((through[:, None, None] * incoming + state, docs_block[-1]), outputs)
    initial = (jnp.zeros((NH, P_SIZE, NS), jnp.float32), jnp.array(-1, jnp.int32))
    final_carry, ssm_blocks = lax.scan(advance, initial, (blocks_conv, blocks_step, blocks_doc))
    ssm_out = ssm_blocks.reshape(TOKENS, INNER)
    gated = (ssm_out * jax.nn.silu(gate_z.astype(jnp.float32))).reshape(TOKENS, G, INNER // G)
    power = lax.optimization_barrier(jnp.mean(gated * gated, axis=-1, keepdims=True))
    normed_ssm = ((gated * lax.rsqrt(power + epsilon)).reshape(TOKENS, INNER) * norm_gain).astype(jnp.bfloat16)
    projected = jnp.dot(normed_ssm, w_out, preferred_element_type=jnp.float32)
    hidden_out = (residual.astype(jnp.float32) + projected).astype(jnp.bfloat16)
    stream = hidden_out.astype(jnp.float32)
    stream_power = lax.optimization_barrier(jnp.mean(stream * stream, axis=-1, keepdims=True))
    normed = (stream * lax.rsqrt(stream_power + epsilon) * attn_gain).astype(jnp.bfloat16)
    positions = jnp.arange(TOKENS, dtype=jnp.int32)
    queries = rotate(jnp.dot(normed, w_query, preferred_element_type=jnp.float32), positions).astype(jnp.bfloat16)
    key_matrix = rotate(jnp.dot(normed, w_key, preferred_element_type=jnp.float32), positions).astype(jnp.bfloat16)
    value_matrix = jnp.dot(normed, value_weight, preferred_element_type=jnp.float32).astype(jnp.bfloat16)
    attention_window = min(DOC_MOST + TOK_DEV, TOKENS)
    scaling = HEAD_DIMENSION ** (-0.5)

    def attend_block(block_index):
        q_start = (block_index * TOK_DEV).astype(jnp.int32)
        key_begin = jnp.clip(q_start + TOK_DEV - attention_window, 0, TOKENS - attention_window).astype(jnp.int32)
        query_rows = lax.dynamic_slice_in_dim(queries, q_start, TOK_DEV).reshape(TOK_DEV, QUERY_HEADS, HEAD_DIMENSION).astype(jnp.float32)
        key_row_block = jnp.repeat(lax.dynamic_slice_in_dim(key_matrix, key_begin, attention_window).reshape(attention_window, KEY_VALUE_HEADS, HEAD_DIMENSION).astype(jnp.float32), QUERY_HEADS // KEY_VALUE_HEADS, axis=1)
        value_row_block = jnp.repeat(lax.dynamic_slice_in_dim(value_matrix, key_begin, attention_window).reshape(attention_window, KEY_VALUE_HEADS, HEAD_DIMENSION).astype(jnp.float32), QUERY_HEADS // KEY_VALUE_HEADS, axis=1)
        query_doc = lax.dynamic_slice_in_dim(doc_ids, q_start, TOK_DEV)
        key_doc = lax.dynamic_slice_in_dim(doc_ids, key_begin, attention_window)
        query_pos = q_start + jnp.arange(TOK_DEV, dtype=jnp.int32)
        key_pos = key_begin + jnp.arange(attention_window, dtype=jnp.int32)
        allowed = (query_doc[:, None] == key_doc[None, :]) & (key_pos[None, :] <= query_pos[:, None])
        scores = jnp.einsum('thd,shd->hts', query_rows, key_row_block, precision=lax.Precision.HIGHEST) * scaling
        masked_scores = jnp.where(allowed[None], scores, -jnp.inf)
        highest = lax.optimization_barrier(jnp.max(masked_scores, axis=-1, keepdims=True))
        expd = jnp.exp(masked_scores - highest)
        denom = lax.optimization_barrier(jnp.sum(expd, axis=-1))
        probs = lax.optimization_barrier(expd.astype(jnp.bfloat16)).astype(jnp.float32)
        output_rows = jnp.einsum('hts,shd->thd', probs, value_row_block, precision=lax.Precision.HIGHEST) / denom.T[:, :, None]
        return output_rows.reshape(TOK_DEV, QUERY_HEADS * HEAD_DIMENSION).astype(jnp.bfloat16)
    context = lax.map(attend_block, jnp.arange(N_CONTEXT, dtype=jnp.int32)).reshape(TOKENS, QUERY_HEADS * HEAD_DIMENSION)
    device_ids = jnp.arange(N_CONTEXT, dtype=jnp.int32)
    inverse = lax.optimization_barrier(jnp.sum(jnp.where(owners[:, None, :] == device_ids[None, :, None], device_ids[None, None, :], 0), axis=2))
    row_starts = device_ids[None, :] * TOK_DEV + inverse.T * QBLK
    row_index = (row_starts[:, :, None] + jnp.arange(QBLK, dtype=jnp.int32)[None, None, :]).reshape(TOKENS)
    attended = jnp.take(context, row_index, axis=0)
    return (hidden_out, attended)
```

```python
import math

import jax
import jax.numpy as jnp
from jax import lax
from jax.experimental import pallas as pl
from jax.experimental.pallas import tpu as pltpu
from jax.sharding import PartitionSpec as P

P_SIZE = 64
NS = 128
HEAD_DIMENSION = 128
N_CTX = 32
N_Y = 4
N_Z = 8
N_T = 4
WINDOW = 18

epsilon = 1e-05
rope_base = 500000.0
MESH = pl.DeviceIdType.MESH
VMEM = pltpu.VMEM
DMA = pltpu.SemaphoreType.DMA


def context_peer(index):
    return {"context": index}


def tensor_peer(index):
    return {"tensor": index}


def remote(src, dst, send_sem, recv_sem, peer):
    return pltpu.make_async_remote_copy(
        src_ref=src,
        dst_ref=dst,
        send_sem=send_sem,
        recv_sem=recv_sem,
        device_id=peer,
        device_id_type=MESH,
    )


def barrier_context(me):
    barrier = pltpu.get_barrier_semaphore()

    def signal(step, carry):
        pl.semaphore_signal(
            barrier,
            inc=1,
            device_id=context_peer(lax.rem(me + step, N_CTX)),
            device_id_type=MESH,
        )
        return carry

    lax.fori_loop(1, N_CTX, signal, 0)
    return barrier


def state_kernel(
    pieces, side, incoming, side_out, recv, scanned, send1, recv1, send2, recv2, send3, recv3
):
    me = lax.axis_index("context")
    barrier = barrier_context(me)
    recv[me] = pieces[me]
    side_out[me] = side[me]
    pl.semaphore_wait(barrier, N_CTX - 1)

    def piece_copy(target, slot, step):
        return remote(
            pieces.at[target], recv.at[slot], send1.at[step], recv1.at[slot], context_peer(target)
        )

    def side_copy(target, slot, step):
        return remote(
            side.at[target], side_out.at[slot], send2.at[step], recv2.at[slot], context_peer(target)
        )

    def back_copy(target, slot, step):
        return remote(
            scanned.at[target], incoming.at[slot], send3.at[step], recv3.at[slot], context_peer(target)
        )

    def start_out(step, carry):
        target = lax.rem(me + step, N_CTX)
        side_copy(target, me, step).start()
        piece_copy(target, me, step).start()
        return carry

    lax.fori_loop(1, N_CTX, start_out, 0)

    def arrive(step, carry):
        source = lax.rem(me + step, N_CTX)
        side_copy(source, source, step).wait_recv()
        piece_copy(source, source, step).wait_recv()
        return carry

    lax.fori_loop(1, N_CTX, arrive, 0)

    def one(turn, state):
        scanned[turn] = state.astype(jnp.bfloat16)
        return state * side_out[turn, 2:3, :] + recv[turn].astype(jnp.float32)

    lax.fori_loop(0, N_CTX, one, jnp.zeros(recv.shape[1:], jnp.float32))
    incoming[me] = scanned[me]

    def start_back(step, carry):
        back_copy(lax.rem(me + step, N_CTX), me, step).start()
        return carry

    lax.fori_loop(1, N_CTX, start_back, 0)

    def finish(step, carry):
        source = lax.rem(me + step, N_CTX)
        back_copy(source, source, step).wait_recv()
        piece_copy(source, source, step).wait_send()
        side_copy(source, source, step).wait_send()
        back_copy(source, source, step).wait_send()
        return carry

    lax.fori_loop(1, N_CTX, finish, 0)


def exchange_state(pieces, side):
    shape = pieces.shape
    spec = pl.BlockSpec(memory_space=VMEM)
    return pl.pallas_call(
        state_kernel,
        out_shape=(
            jax.ShapeDtypeStruct(shape, jnp.bfloat16),
            jax.ShapeDtypeStruct(side.shape, jnp.float32),
        ),
        in_specs=[spec, spec],
        out_specs=(spec, spec),
        scratch_shapes=[
            VMEM(shape, jnp.bfloat16),
            VMEM(shape, jnp.bfloat16),
        ]
        + [DMA((N_CTX,))] * 6,
        compiler_params=pltpu.CompilerParams(collective_id=0, has_side_effects=True),
        name="state_exchange",
    )(pieces, side)


def project_kernel(
    normed,
    w_out,
    residual,
    gain,
    weights,
    cosine,
    sine,
    hidden_ref,
    qkv_ref,
    w_tiles,
    relay_a,
    relay_b,
    accum_a,
    accum_b,
    direct_a,
    direct_b,
    stage,
    hold_a,
    hold_b,
    full,
    gathered,
    load_sem,
    rs_send,
    rs_recv,
    ag_send,
    ag_recv,
    z_send,
    z_recv,
    y_send,
    y_recv,
    core_send,
    core_recv,
):
    me = lax.axis_index("tensor")
    place = lax.axis_index("context")
    core = lax.axis_index("dp")
    other = 1 - core
    right = lax.rem(me + 1, N_T)
    left = lax.rem(me + 3, N_T)
    opposite = lax.rem(me + 2, N_T)
    row = lax.div(place, N_Z)
    col = lax.rem(place, N_Z)
    up = lax.rem(row + 1, N_Y)
    down = lax.rem(row + 3, N_Y)
    far = lax.rem(row + 2, N_Y)
    half = normed.shape[0] // 2
    width = residual.shape[1]

    barrier = pltpu.get_barrier_semaphore()
    for peer in (
        tensor_peer(right),
        tensor_peer(left),
        context_peer(up * N_Z + col),
        context_peer(down * N_Z + col),
        {"dp": other},
    ):
        pl.semaphore_signal(barrier, inc=1, device_id=peer, device_id_type=MESH)
    for step in range(1, N_Z):
        pl.semaphore_signal(
            barrier,
            inc=1,
            device_id=context_peer(row * N_Z + lax.rem(col + step, N_Z)),
            device_id_type=MESH,
        )

    order = (opposite, right, left, me)

    def tile_load(number):
        column = pl.multiple_of(order[number] * width, width)
        return pltpu.make_async_copy(
            w_out.at[:, pl.ds(column, width)], w_tiles.at[number], load_sem.at[number]
        )

    for number in range(N_T):
        tile_load(number).start()
    gathered[place, core] = weights[core]

    def multiply(number):
        tile_load(number).wait()
        return jnp.dot(normed[...], w_tiles[number], preferred_element_type=jnp.float32)

    product = multiply(0)
    stage[0] = product[:half].astype(jnp.bfloat16)
    stage[1] = product[half:].astype(jnp.bfloat16)

    pl.semaphore_wait(barrier, 5 + N_Z - 1)

    rs = [
        remote(stage.at[0], relay_a, rs_send.at[0], rs_recv.at[0], tensor_peer(right)),
        remote(stage.at[1], relay_b, rs_send.at[1], rs_recv.at[1], tensor_peer(left)),
        remote(stage.at[2], direct_b, rs_send.at[2], rs_recv.at[2], tensor_peer(right)),
        remote(stage.at[3], direct_a, rs_send.at[3], rs_recv.at[3], tensor_peer(left)),
        remote(stage.at[4], accum_a, rs_send.at[4], rs_recv.at[4], tensor_peer(right)),
        remote(stage.at[5], accum_b, rs_send.at[5], rs_recv.at[5], tensor_peer(left)),
    ]
    rs[0].start()
    rs[1].start()

    def z_copy(step):
        target = row * N_Z + lax.rem(col + step, N_Z)
        return remote(
            weights.at[core],
            gathered.at[place, core],
            z_send.at[step],
            z_recv.at[step],
            context_peer(target),
        )

    for step in (1, 7, 2, 6, 3, 5, 4):
        z_copy(step).start()

    product = multiply(1)
    stage[2] = product[half:].astype(jnp.bfloat16)
    hold_a[...] = product[:half]
    rs[2].start()
    product = multiply(2)
    stage[3] = product[:half].astype(jnp.bfloat16)
    hold_b[...] = product[half:]
    rs[3].start()
    rs[0].wait_recv()
    stage[4] = (hold_a[...] + relay_a[...].astype(jnp.float32)).astype(jnp.bfloat16)
    rs[4].start()
    rs[1].wait_recv()
    stage[5] = (hold_b[...] + relay_b[...].astype(jnp.float32)).astype(jnp.bfloat16)
    rs[5].start()
    product = multiply(3)
    hold_a[...] = product[:half]
    hold_b[...] = product[half:]
    rs[3].wait_recv()
    rs[4].wait_recv()
    hidden_a = (
        residual[:half].astype(jnp.float32)
        + (
            hold_a[...]
            + (direct_a[...].astype(jnp.float32) + accum_a[...].astype(jnp.float32))
        )
    ).astype(jnp.bfloat16)
    full[me, 0] = hidden_a
    hidden_ref[:half] = hidden_a
    rs[2].wait_recv()
    rs[5].wait_recv()
    hidden_b = (
        residual[half:].astype(jnp.float32)
        + (
            hold_b[...]
            + (direct_b[...].astype(jnp.float32) + accum_b[...].astype(jnp.float32))
        )
    ).astype(jnp.bfloat16)
    full[me, 1] = hidden_b
    hidden_ref[half:] = hidden_b

    def full_copy(owner, part, number, target):
        return remote(
            full.at[owner, part],
            full.at[owner, part],
            ag_send.at[number],
            ag_recv.at[number],
            tensor_peer(target),
        )

    full_copy(me, 0, 0, right).start()
    full_copy(me, 1, 3, left).start()
    full_copy(me, 1, 1, right).start()
    full_copy(me, 0, 2, left).start()

    for step in range(1, N_Z):
        z_copy(step).wait_recv()

    def row_copy(owner_row, begin, count, number, target_row):
        return remote(
            gathered.at[pl.ds(owner_row * N_Z + begin, count), core],
            gathered.at[pl.ds(owner_row * N_Z + begin, count), core],
            y_send.at[number],
            y_recv.at[number],
            context_peer(target_row * N_Z + col),
        )

    quarter = N_Z // 2
    row_copy(row, 0, N_Z, 0, up).start()
    row_copy(row, 0, N_Z, 1, down).start()

    def core_copy(owner_row, number):
        return remote(
            gathered.at[pl.ds(owner_row * N_Z, N_Z), core],
            gathered.at[pl.ds(owner_row * N_Z, N_Z), core],
            core_send.at[number],
            core_recv.at[number],
            {"dp": other},
        )

    def core_arrival(owner_row, number):
        return remote(
            gathered.at[pl.ds(owner_row * N_Z, N_Z), other],
            gathered.at[pl.ds(owner_row * N_Z, N_Z), other],
            core_send.at[number],
            core_recv.at[number],
            {"dp": other},
        )

    core_copy(row, 0).start()

    full_copy(left, 0, 0, right).wait_recv()
    full_copy(left, 0, 4, right).start()
    full_copy(right, 1, 3, left).wait_recv()
    full_copy(right, 1, 5, left).start()

    row_copy(down, 0, N_Z, 0, up).wait_recv()
    row_copy(down, 0, quarter, 2, up).start()
    core_copy(down, 1).start()
    row_copy(up, 0, N_Z, 1, down).wait_recv()
    row_copy(up, quarter, quarter, 3, down).start()
    core_copy(up, 2).start()

    full_copy(left, 1, 1, right).wait_recv()
    full_copy(right, 0, 2, left).wait_recv()
    full_copy(opposite, 0, 4, right).wait_recv()
    full_copy(opposite, 1, 5, left).wait_recv()

    row_copy(far, 0, quarter, 2, up).wait_recv()
    row_copy(far, quarter, quarter, 3, down).wait_recv()
    core_copy(far, 3).start()

    core_arrival(row, 0).wait_recv()
    core_arrival(down, 1).wait_recv()
    core_arrival(up, 2).wait_recv()
    core_arrival(far, 3).wait_recv()

    rows_each = gathered.shape[0] // N_T
    depth = rows_each * gathered.shape[1] * gathered.shape[2]
    for part in range(2):
        squares = jnp.zeros((half, 1), jnp.float32)
        for owner in range(N_T):
            stream = full[owner, part].astype(jnp.float32)
            squares = squares + jnp.sum(stream * stream, axis=1, keepdims=True)
        scale = lax.rsqrt(squares / (N_T * width) + epsilon)
        total = jnp.zeros((half, qkv_ref.shape[1]), jnp.float32)
        for owner in range(N_T):
            stream = full[owner, part].astype(jnp.float32)
            block = (stream * scale * gain[:, owner * width : (owner + 1) * width]).astype(
                jnp.bfloat16
            )
            piece = gathered[owner * rows_each : (owner + 1) * rows_each].reshape(
                depth, gathered.shape[3]
            )
            total = total + jnp.dot(block, piece, preferred_element_type=jnp.float32)
        rows = slice(part * half, (part + 1) * half)
        count = total.shape[1] // HEAD_DIMENSION
        for head in range(count):
            lanes = slice(head * HEAD_DIMENSION, (head + 1) * HEAD_DIMENSION)
            value = total[:, lanes]
            if head < count - 1:
                value = value * cosine[rows] + pltpu.roll(value, HEAD_DIMENSION // 2, 1) * sine[rows]
            qkv_ref[rows, lanes] = value.astype(jnp.bfloat16)

    for copy in rs:
        copy.wait_send()
    full_copy(me, 0, 0, right).wait_send()
    full_copy(me, 1, 3, left).wait_send()
    full_copy(me, 1, 1, right).wait_send()
    full_copy(me, 0, 2, left).wait_send()
    full_copy(left, 0, 4, right).wait_send()
    full_copy(right, 1, 5, left).wait_send()
    for step in range(1, N_Z):
        z_copy(step).wait_send()
    row_copy(row, 0, N_Z, 0, up).wait_send()
    row_copy(row, 0, N_Z, 1, down).wait_send()
    row_copy(down, 0, quarter, 2, up).wait_send()
    row_copy(up, quarter, quarter, 3, down).wait_send()
    core_copy(row, 0).wait_send()
    core_copy(down, 1).wait_send()
    core_copy(up, 2).wait_send()
    core_copy(far, 3).wait_send()


def project(normed, w_out, residual, gain, weights, cosine, sine):
    rows, width = residual.shape
    half = rows // 2
    out_width = weights.shape[2]
    spec = pl.BlockSpec(memory_space=VMEM)
    piece = VMEM((half, width), jnp.bfloat16)
    return pl.pallas_call(
        project_kernel,
        out_shape=(
            jax.ShapeDtypeStruct((rows, width), jnp.bfloat16),
            jax.ShapeDtypeStruct((rows, out_width), jnp.bfloat16),
        ),
        in_specs=[spec, pl.BlockSpec(memory_space=pl.ANY)] + [spec] * 5,
        out_specs=(spec, spec),
        scratch_shapes=[
            VMEM((N_T, width, width), jnp.bfloat16),
            piece,
            piece,
            piece,
            piece,
            piece,
            piece,
            VMEM((6, half, width), jnp.bfloat16),
            VMEM((half, width), jnp.float32),
            VMEM((half, width), jnp.float32),
            VMEM((N_T, 2, half, width), jnp.bfloat16),
            VMEM((N_CTX,) + weights.shape, jnp.bfloat16),
            DMA((N_T,)),
            DMA((6,)),
            DMA((6,)),
            DMA((6,)),
            DMA((6,)),
            DMA((N_Z,)),
            DMA((N_Z,)),
            DMA((4,)),
            DMA((4,)),
            DMA((4,)),
            DMA((4,)),
        ],
        compiler_params=pltpu.CompilerParams(
            collective_id=1, has_side_effects=True, vmem_limit_bytes=56 * 1024 * 1024
        ),
        name="project",
    )(normed, w_out, residual, gain, weights, cosine, sine)


def attend_kernel(
    chosen,
    queries,
    keys_values,
    query_docs,
    key_docs,
    out_ref,
    window,
    rows_buf,
    outgoing,
    best_ref,
    denom_ref,
    accum_ref,
    send_sem,
    recv_sem,
    out_send,
    out_recv,
):
    me = lax.axis_index("context")
    barrier = barrier_context(me)
    window[0] = keys_values[...]
    number = queries.shape[0]
    tokens = keys_values.shape[0]
    group = number // tokens
    scale = HEAD_DIMENSION ** (-0.5)

    def attend(slot):
        keys = window[slot, :, :HEAD_DIMENSION]
        values = window[slot, :, HEAD_DIMENSION:]
        scores = scale * lax.dot_general(
            queries[...], keys, (((1,), (1,)), ((), ())), preferred_element_type=jnp.float32
        )
        usable = query_docs[...] == key_docs[slot]
        if slot == 0:
            q_index = lax.broadcasted_iota(jnp.int32, (group, tokens, tokens), 1).reshape(
                number, tokens
            )
            k_index = lax.broadcasted_iota(jnp.int32, (number, tokens), 1)
            usable = usable & (k_index <= q_index)
        scores = jnp.where(usable, scores, -1e30)
        top = jnp.max(scores, axis=1, keepdims=True)
        if slot == 0:
            probs = jnp.exp(scores - top)
            best_ref[...] = jnp.broadcast_to(top, best_ref.shape)
            denom_ref[...] = jnp.broadcast_to(
                jnp.sum(probs, axis=1, keepdims=True), denom_ref.shape
            )
            accum_ref[...] = jnp.dot(
                probs.astype(jnp.bfloat16), values, preferred_element_type=jnp.float32
            )
        else:
            before = best_ref[...]
            fresh = jnp.maximum(before, top)
            fade = jnp.exp(before - fresh)
            probs = jnp.exp(scores - fresh[:, :1])
            best_ref[...] = fresh
            denom_ref[...] = denom_ref[...] * fade + jnp.sum(probs, axis=1, keepdims=True)
            accum_ref[...] = accum_ref[...] * fade + jnp.dot(
                probs.astype(jnp.bfloat16), values, preferred_element_type=jnp.float32
            )

    forward = lax.rem(me + 1, N_CTX)
    backward = lax.rem(me + N_CTX - 1, N_CTX)

    def send(src, dst, sem, target):
        return remote(
            window.at[src], window.at[dst], send_sem.at[sem], recv_sem.at[dst], context_peer(target)
        )

    started = []

    def go(src, dst, target):
        copy = send(src, dst, len(started), target)
        copy.start()
        started.append(copy)

    def arrived(slot):
        remote(
            window.at[slot],
            window.at[slot],
            send_sem.at[0],
            recv_sem.at[slot],
            context_peer(forward),
        ).wait_recv()

    attend(0)
    pl.semaphore_wait(barrier, N_CTX - 1)
    go(0, 8, lax.rem(me + 8, N_CTX))
    go(0, 1, forward)
    go(0, 16, lax.rem(me + 16, N_CTX))

    arrived(8)
    go(8, 9, forward)
    go(8, 7, backward)
    arrived(1)
    go(1, 2, forward)
    attend(8)
    arrived(16)
    go(16, 15, backward)
    go(16, 17, forward)
    attend(1)
    arrived(9)
    go(9, 10, forward)
    arrived(7)
    go(7, 6, backward)
    attend(16)
    arrived(2)
    go(2, 3, forward)
    attend(9)
    arrived(15)
    go(15, 14, backward)
    attend(7)
    attend(2)
    arrived(10)
    go(10, 11, forward)
    arrived(6)
    go(6, 5, backward)
    attend(15)
    arrived(3)
    go(3, 4, forward)
    attend(10)
    arrived(14)
    go(14, 13, backward)
    attend(6)
    attend(3)
    arrived(13)
    go(13, 12, backward)
    attend(14)
    arrived(17)
    attend(17)
    attend(13)
    arrived(11)
    attend(11)
    arrived(5)
    attend(5)
    arrived(4)
    attend(4)
    arrived(12)
    attend(12)

    result = accum_ref[...] / denom_ref[...]
    for head in range(group):
        lanes = slice(head * HEAD_DIMENSION, (head + 1) * HEAD_DIMENSION)
        rows_buf[:, :, lanes] = (
            result[head * tokens : (head + 1) * tokens]
            .reshape(N_CTX, tokens // N_CTX, HEAD_DIMENSION)
            .astype(jnp.bfloat16)
        )

    def place_row(index, carry):
        outgoing[index] = rows_buf[chosen[index]]
        return carry

    lax.fori_loop(0, N_CTX, place_row, 0)
    out_ref[me] = outgoing[me]

    def row_copy(target, slot, step):
        return remote(
            outgoing.at[target],
            out_ref.at[slot],
            out_send.at[step],
            out_recv.at[slot],
            context_peer(target),
        )

    def start_rows(step, carry):
        row_copy(lax.rem(me + step, N_CTX), me, step).start()
        return carry

    lax.fori_loop(1, N_CTX, start_rows, 0)
    for copy in started:
        copy.wait_send()

    def finish(step, carry):
        source = lax.rem(me + step, N_CTX)
        row_copy(source, source, step).wait_recv()
        row_copy(source, source, step).wait_send()
        return carry

    lax.fori_loop(1, N_CTX, finish, 0)


def attend(chosen, queries, keys_values, query_docs, key_docs):
    number = queries.shape[0]
    tokens, pair = keys_values.shape
    out_width = number // tokens * HEAD_DIMENSION
    spec = pl.BlockSpec(memory_space=VMEM)
    rows = (N_CTX, tokens // N_CTX, out_width)
    return pl.pallas_call(
        attend_kernel,
        out_shape=jax.ShapeDtypeStruct(rows, jnp.bfloat16),
        in_specs=[pl.BlockSpec(memory_space=pltpu.SMEM)] + [spec] * 4,
        out_specs=spec,
        scratch_shapes=[
            VMEM((WINDOW, tokens, pair), jnp.bfloat16),
            VMEM(rows, jnp.bfloat16),
            VMEM(rows, jnp.bfloat16),
            VMEM((number, HEAD_DIMENSION), jnp.float32),
            VMEM((number, HEAD_DIMENSION), jnp.float32),
            VMEM((number, HEAD_DIMENSION), jnp.float32),
            DMA((WINDOW,)),
            DMA((WINDOW,)),
            DMA((N_CTX,)),
            DMA((N_CTX,)),
        ],
        compiler_params=pltpu.CompilerParams(
            collective_id=2, has_side_effects=True, vmem_limit_bytes=48 * 1024 * 1024
        ),
        name="attend",
    )(chosen, queries, keys_values, query_docs, key_docs)


def per_device(
    mixer_input,
    gate_z,
    dt_raw,
    dt_bias,
    a_log,
    d_skip,
    conv_weight,
    conv_bias,
    norm_gain,
    w_out,
    residual,
    attn_gain,
    w_query,
    w_key,
    value_weight,
    doc_ids,
    owners,
):
    row_count = mixer_input.shape[0]
    position_here = lax.axis_index("context")
    first_row = position_here * row_count
    lag = conv_weight.shape[0] - 1
    channels = mixer_input.shape[1]
    last_rows = jnp.concatenate(
        [
            mixer_input[row_count - lag :],
            jnp.broadcast_to(
                doc_ids[row_count - lag :, None].astype(jnp.bfloat16), (lag, HEAD_DIMENSION)
            ),
        ],
        axis=1,
    )
    before = lax.ppermute(
        last_rows, "context", [(source, source + 1) for source in range(N_CTX - 1)]
    )
    before_rows = before[:, :channels]
    before_docs = jnp.where(position_here > 0, before[:, channels].astype(jnp.int32), -1)
    prev_doc = before_docs[lag - 1]
    extended = jnp.concatenate([before_rows, mixer_input]).astype(jnp.float32)
    extended_docs = jnp.concatenate([before_docs, doc_ids])
    running = jnp.broadcast_to(conv_bias, mixer_input.shape)
    for offset in range(lag + 1):
        same_doc = extended_docs[offset : offset + row_count] == doc_ids
        running = running + conv_weight[offset] * jnp.where(
            same_doc[:, None], extended[offset : offset + row_count], 0.0
        )
    conv_out = jax.nn.silu(running).astype(jnp.bfloat16)
    heads = dt_raw.shape[1]
    width_x = heads * P_SIZE
    inputs_x = conv_out[:, :width_x].reshape(row_count, heads, P_SIZE)
    in_b = conv_out[:, width_x : width_x + NS]
    out_c = conv_out[:, width_x + NS :]
    step_size = jax.nn.softplus(dt_raw + dt_bias)
    cumul = jnp.cumsum(-step_size * jnp.exp(a_log), axis=0)
    intersection = lax.dot_general(
        out_c, in_b, (((1,), (1,)), ((), ())), preferred_element_type=jnp.float32
    )
    row_ids = jnp.arange(row_count, dtype=jnp.int32)
    allowed = (doc_ids[:, None] == doc_ids[None, :]) & (row_ids[:, None] >= row_ids[None, :])
    decays = jnp.exp(jnp.where(allowed[None], cumul.T[:, :, None] - cumul.T[:, None, :], -jnp.inf))
    weights = decays * intersection[None] * step_size.T[:, None, :]
    inputs_float = inputs_x.astype(jnp.float32)
    outputs = jnp.einsum("hts,shp->thp", weights, inputs_float, precision=lax.Precision.HIGHEST)
    end_weight = (
        jnp.exp(cumul[-1][None, :] - cumul)
        * (doc_ids == doc_ids[-1]).astype(jnp.float32)[:, None]
        * step_size
    )
    state = jnp.einsum(
        "sh,shp,sn->hpn",
        end_weight,
        inputs_float,
        in_b.astype(jnp.float32),
        precision=lax.Precision.HIGHEST,
    )
    through = jnp.exp(cumul[-1]) * (doc_ids[-1] == prev_doc).astype(jnp.float32)

    pieces = state.astype(jnp.bfloat16).reshape(N_CTX, heads * P_SIZE // N_CTX, NS)
    docs_rows = doc_ids.astype(jnp.float32).reshape(row_count // NS, NS)
    side = jnp.concatenate(
        [
            jnp.broadcast_to(docs_rows[None], (N_CTX,) + docs_rows.shape),
            jnp.broadcast_to(
                jnp.repeat(through, N_CTX // heads)[:, None, None],
                (N_CTX, 8 - docs_rows.shape[0], NS),
            ),
        ],
        axis=1,
    )
    incoming_pieces, side_all = exchange_state(pieces, side)
    incoming = incoming_pieces.reshape(heads, P_SIZE, NS)
    all_docs = side_all[:, : docs_rows.shape[0]].reshape(N_CTX, row_count)

    carry_on = (doc_ids == prev_doc).astype(jnp.float32)
    outputs = outputs + jnp.exp(cumul)[:, :, None] * carry_on[:, None, None] * jnp.einsum(
        "tn,hpn->thp", out_c, incoming, preferred_element_type=jnp.float32
    )
    outputs = outputs + d_skip[None, :, None] * inputs_float
    gated = outputs.reshape(row_count, width_x) * jax.nn.silu(gate_z.astype(jnp.float32))
    power = jnp.mean(gated * gated, axis=-1, keepdims=True)
    normed_ssm = (gated * lax.rsqrt(power + epsilon) * norm_gain).astype(jnp.bfloat16)

    shard = jnp.concatenate([w_query, w_key, value_weight], axis=1)
    shard = shard.reshape(2, shard.shape[0] // 2, shard.shape[1])
    positions = first_row + jnp.arange(row_count, dtype=jnp.int32)
    half_width = HEAD_DIMENSION // 2
    freqs = jnp.exp(
        jnp.arange(half_width, dtype=jnp.float32) * (-2.0 * math.log(rope_base) / HEAD_DIMENSION)
    )
    angles = positions.astype(jnp.float32)[:, None] * freqs[None, :]
    cosine = jnp.cos(angles)
    sine = jnp.sin(angles)
    cosine = jnp.concatenate([cosine, cosine], axis=1)
    sine = jnp.concatenate([-sine, sine], axis=1)
    hidden_out, qkv = project(
        normed_ssm, w_out, residual, attn_gain[None, :], shard, cosine, sine
    )
    query_width = w_query.shape[1]
    group = query_width // HEAD_DIMENSION
    queries = (
        qkv[:, :query_width]
        .reshape(row_count, group, HEAD_DIMENSION)
        .transpose(1, 0, 2)
        .reshape(group * row_count, HEAD_DIMENSION)
    )
    device_ids = jnp.arange(N_CTX, dtype=jnp.int32)
    chosen = jnp.sum(
        jnp.where(owners[0][None, :] == device_ids[:, None], device_ids[None, :], 0), axis=1
    )
    blocks = position_here - jnp.arange(WINDOW, dtype=jnp.int32)
    key_docs = jnp.where(
        (blocks >= 0)[:, None], jnp.take(all_docs, jnp.mod(blocks, N_CTX), axis=0), -1.0
    )[:, None, :]
    query_docs = jnp.tile(doc_ids.astype(jnp.float32), group)[:, None]
    attended = attend(chosen, queries, qkv[:, query_width:], query_docs, key_docs)
    return (hidden_out, attended.reshape(row_count, query_width))


def solution(mesh):
    in_specs = (
        P(("dp", "context"), "tensor"),
        P(("dp", "context"), "tensor"),
        P(("dp", "context"), "tensor"),
        P("tensor"),
        P("tensor"),
        P("tensor"),
        P(None, "tensor"),
        P("tensor"),
        P("tensor"),
        P("tensor", None),
        P(("dp", "context"), "tensor"),
        P(),
        P("context", "tensor"),
        P("context", "tensor"),
        P("context", "tensor"),
        P(("dp", "context")),
        P(("dp", "context"), None),
    )
    out_specs = (P(("dp", "context"), "tensor"), P(("dp", "context"), "tensor"))
    return jax.shard_map(
        per_device, mesh=mesh, in_specs=in_specs, out_specs=out_specs, check_vma=False
    )
```

```python
import math

import jax
import jax.numpy as jnp
from jax import lax
from jax.experimental import pallas as pl
from jax.experimental.pallas import tpu as pltpu
from jax.sharding import PartitionSpec as P

P_SIZE = 64
NS = 128
HEAD_DIMENSION = 128
N_CTX = 32
N_Y = 4
N_Z = 8
N_T = 4
WINDOW = 18
DOCS = 16

epsilon = 1e-05
rope_base = 500000.0
MESH = pl.DeviceIdType.MESH
VMEM = pltpu.VMEM
DMA = pltpu.SemaphoreType.DMA


def context_peer(index):
    return {"context": index}


def tensor_peer(index):
    return {"tensor": index}


def remote(src, dst, send_sem, recv_sem, peer):
    return pltpu.make_async_remote_copy(
        src_ref=src,
        dst_ref=dst,
        send_sem=send_sem,
        recv_sem=recv_sem,
        device_id=peer,
        device_id_type=MESH,
    )


def barrier_context(me):
    barrier = pltpu.get_barrier_semaphore()

    def signal(step, carry):
        pl.semaphore_signal(
            barrier,
            inc=1,
            device_id=context_peer(lax.rem(me + step, N_CTX)),
            device_id_type=MESH,
        )
        return carry

    lax.fori_loop(1, N_CTX, signal, 0)
    return barrier


def state_kernel(
    pieces, side, incoming, side_out, recv, scanned, send1, recv1, send2, recv2, send3, recv3
):
    me = lax.axis_index("context")
    barrier = barrier_context(me)
    recv[me] = pieces[me]
    side_out[me] = side[me]
    pl.semaphore_wait(barrier, N_CTX - 1)

    def piece_copy(target, slot, step):
        return remote(
            pieces.at[target], recv.at[slot], send1.at[step], recv1.at[slot], context_peer(target)
        )

    def side_copy(target, slot, step):
        return remote(
            side.at[target], side_out.at[slot], send2.at[step], recv2.at[slot], context_peer(target)
        )

    def back_copy(target, slot, step):
        return remote(
            scanned.at[target], incoming.at[slot], send3.at[step], recv3.at[slot], context_peer(target)
        )

    def start_out(step, carry):
        target = lax.rem(me + step, N_CTX)
        side_copy(target, me, step).start()
        piece_copy(target, me, step).start()
        return carry

    lax.fori_loop(1, N_CTX, start_out, 0)

    def arrive(step, carry):
        source = lax.rem(me + step, N_CTX)
        side_copy(source, source, step).wait_recv()
        piece_copy(source, source, step).wait_recv()
        return carry

    lax.fori_loop(1, N_CTX, arrive, 0)

    def one(turn, state):
        scanned[turn] = state.astype(jnp.bfloat16)
        return state * side_out[turn, 2:3, :] + recv[turn].astype(jnp.float32)

    lax.fori_loop(0, N_CTX, one, jnp.zeros(recv.shape[1:], jnp.float32))
    incoming[me] = scanned[me]

    def start_back(step, carry):
        back_copy(lax.rem(me + step, N_CTX), me, step).start()
        return carry

    lax.fori_loop(1, N_CTX, start_back, 0)

    def finish(step, carry):
        source = lax.rem(me + step, N_CTX)
        back_copy(source, source, step).wait_recv()
        piece_copy(source, source, step).wait_send()
        side_copy(source, source, step).wait_send()
        back_copy(source, source, step).wait_send()
        return carry

    lax.fori_loop(1, N_CTX, finish, 0)


def exchange_state(pieces, side):
    shape = pieces.shape
    spec = pl.BlockSpec(memory_space=VMEM)
    return pl.pallas_call(
        state_kernel,
        out_shape=(
            jax.ShapeDtypeStruct(shape, jnp.bfloat16),
            jax.ShapeDtypeStruct(side.shape, jnp.float32),
        ),
        in_specs=[spec, spec],
        out_specs=(spec, spec),
        scratch_shapes=[
            VMEM(shape, jnp.bfloat16),
            VMEM(shape, jnp.bfloat16),
        ]
        + [DMA((N_CTX,))] * 6,
        compiler_params=pltpu.CompilerParams(collective_id=0, has_side_effects=True),
        name="state_exchange",
    )(pieces, side)


def project_kernel(
    normed,
    w_out,
    residual,
    gain,
    weights,
    cosine,
    sine,
    hidden_ref,
    query_ref,
    pair_ref,
    w_tiles,
    relay_a,
    relay_b,
    accum_a,
    accum_b,
    direct_a,
    direct_b,
    stage,
    hold_a,
    hold_b,
    full,
    gathered,
    load_sem,
    rs_send,
    rs_recv,
    ag_send,
    ag_recv,
    z_send,
    z_recv,
    y_send,
    y_recv,
    core_send,
    core_recv,
):
    me = lax.axis_index("tensor")
    place = lax.axis_index("context")
    core = lax.axis_index("dp")
    other = 1 - core
    right = lax.rem(me + 1, N_T)
    left = lax.rem(me + 3, N_T)
    opposite = lax.rem(me + 2, N_T)
    row = lax.div(place, N_Z)
    col = lax.rem(place, N_Z)
    up = lax.rem(row + 1, N_Y)
    down = lax.rem(row + 3, N_Y)
    far = lax.rem(row + 2, N_Y)
    half = normed.shape[0] // 2
    width = residual.shape[1]

    barrier = pltpu.get_barrier_semaphore()
    for peer in (
        tensor_peer(right),
        tensor_peer(left),
        context_peer(up * N_Z + col),
        context_peer(down * N_Z + col),
        {"dp": other},
    ):
        pl.semaphore_signal(barrier, inc=1, device_id=peer, device_id_type=MESH)
    for step in range(1, N_Z):
        pl.semaphore_signal(
            barrier,
            inc=1,
            device_id=context_peer(row * N_Z + lax.rem(col + step, N_Z)),
            device_id_type=MESH,
        )

    order = (opposite, right, left, me)

    def tile_load(number):
        column = pl.multiple_of(order[number] * width, width)
        return pltpu.make_async_copy(
            w_out.at[:, pl.ds(column, width)], w_tiles.at[number], load_sem.at[number]
        )

    for number in range(N_T):
        tile_load(number).start()
    gathered[place, core] = weights[core]

    def multiply(number):
        tile_load(number).wait()
        return jnp.dot(normed[...], w_tiles[number], preferred_element_type=jnp.float32)

    product = multiply(0)
    stage[0] = product[:half].astype(jnp.bfloat16)
    stage[1] = product[half:].astype(jnp.bfloat16)

    pl.semaphore_wait(barrier, 5 + N_Z - 1)

    rs = [
        remote(stage.at[0], relay_a, rs_send.at[0], rs_recv.at[0], tensor_peer(right)),
        remote(stage.at[1], relay_b, rs_send.at[1], rs_recv.at[1], tensor_peer(left)),
        remote(stage.at[2], direct_b, rs_send.at[2], rs_recv.at[2], tensor_peer(right)),
        remote(stage.at[3], direct_a, rs_send.at[3], rs_recv.at[3], tensor_peer(left)),
        remote(stage.at[4], accum_a, rs_send.at[4], rs_recv.at[4], tensor_peer(right)),
        remote(stage.at[5], accum_b, rs_send.at[5], rs_recv.at[5], tensor_peer(left)),
    ]
    rs[0].start()
    rs[1].start()

    def z_copy(step):
        target = row * N_Z + lax.rem(col + step, N_Z)
        return remote(
            weights.at[core],
            gathered.at[place, core],
            z_send.at[step],
            z_recv.at[step],
            context_peer(target),
        )

    for step in (1, 7, 2, 6, 3, 5, 4):
        z_copy(step).start()

    product = multiply(1)
    stage[2] = product[half:].astype(jnp.bfloat16)
    hold_a[...] = product[:half]
    rs[2].start()
    product = multiply(2)
    stage[3] = product[:half].astype(jnp.bfloat16)
    hold_b[...] = product[half:]
    rs[3].start()
    rs[0].wait_recv()
    stage[4] = (hold_a[...] + relay_a[...].astype(jnp.float32)).astype(jnp.bfloat16)
    rs[4].start()
    rs[1].wait_recv()
    stage[5] = (hold_b[...] + relay_b[...].astype(jnp.float32)).astype(jnp.bfloat16)
    rs[5].start()
    product = multiply(3)
    hold_a[...] = product[:half]
    hold_b[...] = product[half:]
    rs[3].wait_recv()
    rs[4].wait_recv()
    hidden_a = (
        residual[:half].astype(jnp.float32)
        + (
            hold_a[...]
            + (direct_a[...].astype(jnp.float32) + accum_a[...].astype(jnp.float32))
        )
    ).astype(jnp.bfloat16)
    full[me, 0] = hidden_a
    hidden_ref[:half] = hidden_a
    rs[2].wait_recv()
    rs[5].wait_recv()
    hidden_b = (
        residual[half:].astype(jnp.float32)
        + (
            hold_b[...]
            + (direct_b[...].astype(jnp.float32) + accum_b[...].astype(jnp.float32))
        )
    ).astype(jnp.bfloat16)
    full[me, 1] = hidden_b
    hidden_ref[half:] = hidden_b

    def full_copy(owner, part, number, target):
        return remote(
            full.at[owner, part],
            full.at[owner, part],
            ag_send.at[number],
            ag_recv.at[number],
            tensor_peer(target),
        )

    full_copy(me, 0, 0, right).start()
    full_copy(me, 1, 3, left).start()
    full_copy(me, 1, 1, right).start()
    full_copy(me, 0, 2, left).start()

    for step in range(1, N_Z):
        z_copy(step).wait_recv()

    def row_copy(owner_row, begin, count, number, target_row):
        return remote(
            gathered.at[pl.ds(owner_row * N_Z + begin, count), core],
            gathered.at[pl.ds(owner_row * N_Z + begin, count), core],
            y_send.at[number],
            y_recv.at[number],
            context_peer(target_row * N_Z + col),
        )

    quarter = N_Z // 2
    row_copy(row, 0, N_Z, 0, up).start()
    row_copy(row, 0, N_Z, 1, down).start()

    def core_copy(owner_row, number):
        return remote(
            gathered.at[pl.ds(owner_row * N_Z, N_Z), core],
            gathered.at[pl.ds(owner_row * N_Z, N_Z), core],
            core_send.at[number],
            core_recv.at[number],
            {"dp": other},
        )

    def core_arrival(owner_row, number):
        return remote(
            gathered.at[pl.ds(owner_row * N_Z, N_Z), other],
            gathered.at[pl.ds(owner_row * N_Z, N_Z), other],
            core_send.at[number],
            core_recv.at[number],
            {"dp": other},
        )

    core_copy(row, 0).start()

    full_copy(left, 0, 0, right).wait_recv()
    full_copy(left, 0, 4, right).start()
    full_copy(right, 1, 3, left).wait_recv()
    full_copy(right, 1, 5, left).start()

    row_copy(down, 0, N_Z, 0, up).wait_recv()
    row_copy(down, 0, quarter, 2, up).start()
    core_copy(down, 1).start()
    row_copy(up, 0, N_Z, 1, down).wait_recv()
    row_copy(up, quarter, quarter, 3, down).start()
    core_copy(up, 2).start()

    full_copy(left, 1, 1, right).wait_recv()
    full_copy(right, 0, 2, left).wait_recv()
    full_copy(opposite, 0, 4, right).wait_recv()
    full_copy(opposite, 1, 5, left).wait_recv()

    row_copy(far, 0, quarter, 2, up).wait_recv()
    row_copy(far, quarter, quarter, 3, down).wait_recv()
    core_copy(far, 3).start()

    core_arrival(row, 0).wait_recv()
    core_arrival(down, 1).wait_recv()
    core_arrival(up, 2).wait_recv()
    core_arrival(far, 3).wait_recv()

    rows_each = gathered.shape[0] // N_T
    depth = rows_each * gathered.shape[1] * gathered.shape[2]
    for part in range(2):
        squares = jnp.zeros((half, 1), jnp.float32)
        for owner in range(N_T):
            stream = full[owner, part].astype(jnp.float32)
            squares = squares + jnp.sum(stream * stream, axis=1, keepdims=True)
        scale = lax.rsqrt(squares / (N_T * width) + epsilon)
        total = jnp.zeros((half, weights.shape[2]), jnp.float32)
        for owner in range(N_T):
            stream = full[owner, part].astype(jnp.float32)
            block = (stream * scale * gain[:, owner * width : (owner + 1) * width]).astype(
                jnp.bfloat16
            )
            piece = gathered[owner * rows_each : (owner + 1) * rows_each].reshape(
                depth, gathered.shape[3]
            )
            total = total + jnp.dot(block, piece, preferred_element_type=jnp.float32)
        rows = slice(part * half, (part + 1) * half)
        count = total.shape[1] // HEAD_DIMENSION
        for head in range(count):
            lanes = slice(head * HEAD_DIMENSION, (head + 1) * HEAD_DIMENSION)
            value = total[:, lanes]
            if head < count - 1:
                value = value * cosine[rows] + pltpu.roll(value, HEAD_DIMENSION // 2, 1) * sine[rows]
            if head < count - 2:
                begin = head * 2 * half + part * half
                query_ref[:, begin : begin + half] = value.T.astype(jnp.bfloat16)
            elif head < count - 1:
                pair_ref[rows, :HEAD_DIMENSION] = value.astype(jnp.bfloat16)
            else:
                pair_ref[rows, HEAD_DIMENSION:] = value.T.astype(jnp.bfloat16)

    for copy in rs:
        copy.wait_send()
    full_copy(me, 0, 0, right).wait_send()
    full_copy(me, 1, 3, left).wait_send()
    full_copy(me, 1, 1, right).wait_send()
    full_copy(me, 0, 2, left).wait_send()
    full_copy(left, 0, 4, right).wait_send()
    full_copy(right, 1, 5, left).wait_send()
    for step in range(1, N_Z):
        z_copy(step).wait_send()
    row_copy(row, 0, N_Z, 0, up).wait_send()
    row_copy(row, 0, N_Z, 1, down).wait_send()
    row_copy(down, 0, quarter, 2, up).wait_send()
    row_copy(up, quarter, quarter, 3, down).wait_send()
    core_copy(row, 0).wait_send()
    core_copy(down, 1).wait_send()
    core_copy(up, 2).wait_send()
    core_copy(far, 3).wait_send()


def project(normed, w_out, residual, gain, weights, cosine, sine):
    rows, width = residual.shape
    half = rows // 2
    out_width = weights.shape[2]
    spec = pl.BlockSpec(memory_space=VMEM)
    piece = VMEM((half, width), jnp.bfloat16)
    return pl.pallas_call(
        project_kernel,
        out_shape=(
            jax.ShapeDtypeStruct((rows, width), jnp.bfloat16),
            jax.ShapeDtypeStruct(
                (HEAD_DIMENSION, rows * (out_width // HEAD_DIMENSION - 2)), jnp.bfloat16
            ),
            jax.ShapeDtypeStruct((rows, 2 * HEAD_DIMENSION), jnp.bfloat16),
        ),
        in_specs=[spec, pl.BlockSpec(memory_space=pl.ANY)] + [spec] * 5,
        out_specs=(spec, spec, spec),
        scratch_shapes=[
            VMEM((N_T, width, width), jnp.bfloat16),
            piece,
            piece,
            piece,
            piece,
            piece,
            piece,
            VMEM((6, half, width), jnp.bfloat16),
            VMEM((half, width), jnp.float32),
            VMEM((half, width), jnp.float32),
            VMEM((N_T, 2, half, width), jnp.bfloat16),
            VMEM((N_CTX,) + weights.shape, jnp.bfloat16),
            DMA((N_T,)),
            DMA((6,)),
            DMA((6,)),
            DMA((6,)),
            DMA((6,)),
            DMA((N_Z,)),
            DMA((N_Z,)),
            DMA((4,)),
            DMA((4,)),
            DMA((4,)),
            DMA((4,)),
        ],
        compiler_params=pltpu.CompilerParams(
            collective_id=1, has_side_effects=True, vmem_limit_bytes=56 * 1024 * 1024
        ),
        name="project",
    )(normed, w_out, residual, gain, weights, cosine, sine)


def attend_kernel(
    chosen,
    queries,
    keys_values,
    starts,
    out_ref,
    window,
    rows_buf,
    outgoing,
    best_ref,
    denom_ref,
    accum_ref,
    up_send,
    down_send,
    far_send,
    recv_sem,
    out_send,
    out_recv,
):
    me = lax.axis_index("context")
    barrier = barrier_context(me)
    window[0] = keys_values[...]
    number = queries.shape[1]
    tokens = keys_values.shape[0]
    group = number // tokens
    scale = HEAD_DIMENSION ** (-0.5) / math.log(2.0)

    def masked_scores(slot):
        keys = window[slot, :, :HEAD_DIMENSION]
        scores = scale * jnp.dot(keys, queries[...], preferred_element_type=jnp.float32)
        key_index = lax.broadcasted_iota(jnp.int32, (tokens, number), 0)
        usable = key_index >= starts[...] - tokens * (me - slot)
        return scores, usable, key_index

    def weighted(slot, probs):
        values = jnp.concatenate(
            [
                window[slot, :HEAD_DIMENSION, HEAD_DIMENSION:],
                window[slot, HEAD_DIMENSION:, HEAD_DIMENSION:],
            ],
            axis=1,
        )
        return jnp.dot(values, probs.astype(jnp.bfloat16), preferred_element_type=jnp.float32)

    def attend_first():
        scores, usable, key_index = masked_scores(0)
        query_index = lax.rem(lax.broadcasted_iota(jnp.int32, (1, number), 1), tokens)
        scores = jnp.where(usable & (key_index <= query_index), scores, -1e30)
        top = jnp.max(scores, axis=0, keepdims=True)
        probs = jnp.exp2(scores - top)
        best_ref[...] = top
        denom_ref[...] = jnp.sum(probs, axis=0, keepdims=True)
        accum_ref[...] = weighted(0, probs)

    def attend(slot):
        scores, usable, _ = masked_scores(slot)
        scores = jnp.where(usable, scores, -1e30)
        before = best_ref[...]
        fresh = jnp.maximum(before, jnp.max(scores, axis=0, keepdims=True))
        fade = jnp.exp2(before - fresh)
        probs = jnp.exp2(scores - fresh)
        best_ref[...] = fresh
        denom_ref[...] = denom_ref[...] * fade + jnp.sum(probs, axis=0, keepdims=True)
        accum_ref[...] = accum_ref[...] * fade + weighted(slot, probs)

    forward = lax.rem(me + 1, N_CTX)
    backward = lax.rem(me + N_CTX - 1, N_CTX)

    def send_up(slot):
        return remote(
            window.at[slot],
            window.at[slot + 1],
            up_send.at[slot],
            recv_sem.at[slot + 1],
            context_peer(forward),
        )

    def send_down(slot):
        return remote(
            window.at[slot],
            window.at[slot - 1],
            down_send.at[slot],
            recv_sem.at[slot - 1],
            context_peer(backward),
        )

    def send_far(slot):
        return remote(
            window.at[0],
            window.at[slot],
            far_send.at[slot],
            recv_sem.at[slot],
            context_peer(lax.rem(me + slot, N_CTX)),
        )

    attend_first()
    pl.semaphore_wait(barrier, N_CTX - 1)
    send_far(8).start()
    send_up(0).start()
    send_far(16).start()

    visits = (8, 1, 16, 9, 7, 2, 15, 10, 6, 3, 14, 17, 13, 11, 5, 4, 12)
    goes_up = (1, 2, 3, 8, 9, 10, 16)
    goes_down = (8, 7, 6, 16, 15, 14, 13)

    def visit(step, carry):
        slot = jnp.int32(visits[0])
        for number_here, value in enumerate(visits):
            slot = jnp.where(step == number_here, value, slot)
        send_far(slot).wait_recv()
        upward = ((slot >= 1) & (slot <= 3)) | ((slot >= 8) & (slot <= 10)) | (slot == 16)
        downward = ((slot >= 6) & (slot <= 8)) | ((slot >= 13) & (slot <= 16))

        @pl.when(upward)
        def _():
            send_up(slot).start()

        @pl.when(downward)
        def _():
            send_down(slot).start()

        attend(slot)
        return carry

    lax.fori_loop(0, len(visits), visit, 0)

    result = accum_ref[...] / denom_ref[...]
    for head in range(group):
        lanes = slice(head * HEAD_DIMENSION, (head + 1) * HEAD_DIMENSION)
        rows_buf[:, :, lanes] = (
            result[:, head * tokens : (head + 1) * tokens]
            .T.reshape(N_CTX, tokens // N_CTX, HEAD_DIMENSION)
            .astype(jnp.bfloat16)
        )

    def place_row(index, carry):
        outgoing[index] = rows_buf[chosen[index]]
        return carry

    lax.fori_loop(0, N_CTX, place_row, 0)
    out_ref[me] = outgoing[me]

    def row_copy(target, slot, step):
        return remote(
            outgoing.at[target],
            out_ref.at[slot],
            out_send.at[step],
            out_recv.at[slot],
            context_peer(target),
        )

    def start_rows(step, carry):
        row_copy(lax.rem(me + step, N_CTX), me, step).start()
        return carry

    lax.fori_loop(1, N_CTX, start_rows, 0)
    send_up(0).wait_send()
    for slot in goes_up:
        send_up(slot).wait_send()
    for slot in goes_down:
        send_down(slot).wait_send()
    send_far(8).wait_send()
    send_far(16).wait_send()

    def finish(step, carry):
        source = lax.rem(me + step, N_CTX)
        row_copy(source, source, step).wait_recv()
        row_copy(source, source, step).wait_send()
        return carry

    lax.fori_loop(1, N_CTX, finish, 0)


def attend(chosen, queries, keys_values, starts):
    number = queries.shape[1]
    tokens, pair = keys_values.shape
    out_width = number // tokens * HEAD_DIMENSION
    spec = pl.BlockSpec(memory_space=VMEM)
    rows = (N_CTX, tokens // N_CTX, out_width)
    return pl.pallas_call(
        attend_kernel,
        out_shape=jax.ShapeDtypeStruct(rows, jnp.bfloat16),
        in_specs=[pl.BlockSpec(memory_space=pltpu.SMEM)] + [spec] * 3,
        out_specs=spec,
        scratch_shapes=[
            VMEM((WINDOW, tokens, pair), jnp.bfloat16),
            VMEM(rows, jnp.bfloat16),
            VMEM(rows, jnp.bfloat16),
            VMEM((1, number), jnp.float32),
            VMEM((1, number), jnp.float32),
            VMEM((HEAD_DIMENSION, number), jnp.float32),
            DMA((WINDOW,)),
            DMA((WINDOW,)),
            DMA((WINDOW,)),
            DMA((WINDOW,)),
            DMA((N_CTX,)),
            DMA((N_CTX,)),
        ],
        compiler_params=pltpu.CompilerParams(
            collective_id=2, has_side_effects=True, vmem_limit_bytes=48 * 1024 * 1024
        ),
        name="attend",
    )(chosen, queries, keys_values, starts)


def per_device(
    mixer_input,
    gate_z,
    dt_raw,
    dt_bias,
    a_log,
    d_skip,
    conv_weight,
    conv_bias,
    norm_gain,
    w_out,
    residual,
    attn_gain,
    w_query,
    w_key,
    value_weight,
    doc_ids,
    owners,
):
    row_count = mixer_input.shape[0]
    position_here = lax.axis_index("context")
    first_row = position_here * row_count
    lag = conv_weight.shape[0] - 1
    channels = mixer_input.shape[1]
    last_rows = jnp.concatenate(
        [
            mixer_input[row_count - lag :],
            jnp.broadcast_to(
                doc_ids[row_count - lag :, None].astype(jnp.bfloat16), (lag, HEAD_DIMENSION)
            ),
        ],
        axis=1,
    )
    before = lax.ppermute(
        last_rows, "context", [(source, source + 1) for source in range(N_CTX - 1)]
    )
    before_rows = before[:, :channels]
    before_docs = jnp.where(position_here > 0, before[:, channels].astype(jnp.int32), -1)
    prev_doc = before_docs[lag - 1]
    extended = jnp.concatenate([before_rows, mixer_input]).astype(jnp.float32)
    extended_docs = jnp.concatenate([before_docs, doc_ids])
    running = jnp.broadcast_to(conv_bias, mixer_input.shape)
    for offset in range(lag + 1):
        same_doc = extended_docs[offset : offset + row_count] == doc_ids
        running = running + conv_weight[offset] * jnp.where(
            same_doc[:, None], extended[offset : offset + row_count], 0.0
        )
    conv_out = jax.nn.silu(running).astype(jnp.bfloat16)
    heads = dt_raw.shape[1]
    width_x = heads * P_SIZE
    inputs_x = conv_out[:, :width_x].reshape(row_count, heads, P_SIZE)
    in_b = conv_out[:, width_x : width_x + NS]
    out_c = conv_out[:, width_x + NS :]
    step_size = jax.nn.softplus(dt_raw + dt_bias)
    cumul = jnp.cumsum(-step_size * jnp.exp(a_log), axis=0)
    intersection = lax.dot_general(
        out_c, in_b, (((1,), (1,)), ((), ())), preferred_element_type=jnp.float32
    )
    row_ids = jnp.arange(row_count, dtype=jnp.int32)
    allowed = (doc_ids[:, None] == doc_ids[None, :]) & (row_ids[:, None] >= row_ids[None, :])
    decays = jnp.exp(jnp.where(allowed[None], cumul.T[:, :, None] - cumul.T[:, None, :], -jnp.inf))
    weights = decays * intersection[None] * step_size.T[:, None, :]
    inputs_float = inputs_x.astype(jnp.float32)
    outputs = jnp.einsum("hts,shp->thp", weights, inputs_float, precision=lax.Precision.HIGHEST)
    end_weight = (
        jnp.exp(cumul[-1][None, :] - cumul)
        * (doc_ids == doc_ids[-1]).astype(jnp.float32)[:, None]
        * step_size
    )
    state = jnp.einsum(
        "sh,shp,sn->hpn",
        end_weight,
        inputs_float,
        in_b.astype(jnp.float32),
        precision=lax.Precision.HIGHEST,
    )
    through = jnp.exp(cumul[-1]) * (doc_ids[-1] == prev_doc).astype(jnp.float32)

    pieces = state.astype(jnp.bfloat16).reshape(N_CTX, heads * P_SIZE // N_CTX, NS)
    docs_rows = doc_ids.astype(jnp.float32).reshape(row_count // NS, NS)
    side = jnp.concatenate(
        [
            jnp.broadcast_to(docs_rows[None], (N_CTX,) + docs_rows.shape),
            jnp.broadcast_to(
                jnp.repeat(through, N_CTX // heads)[:, None, None],
                (N_CTX, 8 - docs_rows.shape[0], NS),
            ),
        ],
        axis=1,
    )
    incoming_pieces, side_all = exchange_state(pieces, side)
    incoming = incoming_pieces.reshape(heads, P_SIZE, NS)
    all_docs = side_all[:, : docs_rows.shape[0]].reshape(N_CTX, row_count)

    carry_on = (doc_ids == prev_doc).astype(jnp.float32)
    outputs = outputs + jnp.exp(cumul)[:, :, None] * carry_on[:, None, None] * jnp.einsum(
        "tn,hpn->thp", out_c, incoming, preferred_element_type=jnp.float32
    )
    outputs = outputs + d_skip[None, :, None] * inputs_float
    gated = outputs.reshape(row_count, width_x) * jax.nn.silu(gate_z.astype(jnp.float32))
    power = jnp.mean(gated * gated, axis=-1, keepdims=True)
    normed_ssm = (gated * lax.rsqrt(power + epsilon) * norm_gain).astype(jnp.bfloat16)

    shard = jnp.concatenate([w_query, w_key, value_weight], axis=1)
    shard = shard.reshape(2, shard.shape[0] // 2, shard.shape[1])
    positions = first_row + jnp.arange(row_count, dtype=jnp.int32)
    half_width = HEAD_DIMENSION // 2
    freqs = jnp.exp(
        jnp.arange(half_width, dtype=jnp.float32) * (-2.0 * math.log(rope_base) / HEAD_DIMENSION)
    )
    angles = positions.astype(jnp.float32)[:, None] * freqs[None, :]
    cosine = jnp.cos(angles)
    sine = jnp.sin(angles)
    cosine = jnp.concatenate([cosine, cosine], axis=1)
    sine = jnp.concatenate([-sine, sine], axis=1)
    hidden_out, queries, keys_values = project(
        normed_ssm, w_out, residual, attn_gain[None, :], shard, cosine, sine
    )
    query_width = w_query.shape[1]
    group = query_width // HEAD_DIMENSION
    device_ids = jnp.arange(N_CTX, dtype=jnp.int32)
    chosen = jnp.sum(
        jnp.where(owners[0][None, :] == device_ids[:, None], device_ids[None, :], 0), axis=1
    )
    names = jnp.arange(DOCS, dtype=jnp.int32).astype(jnp.float32)
    doc_starts = jnp.sum(
        (all_docs.reshape(1, -1) < names[:, None]).astype(jnp.int32), axis=1
    )
    starts = jnp.sum(
        jnp.where(
            doc_ids.astype(jnp.float32)[None, :] == names[:, None], doc_starts[:, None], 0
        ),
        axis=0,
    )
    attended = attend(chosen, queries, keys_values, jnp.tile(starts, group)[None, :])
    return (hidden_out, attended.reshape(row_count, query_width))


def solution(mesh):
    in_specs = (
        P(("dp", "context"), "tensor"),
        P(("dp", "context"), "tensor"),
        P(("dp", "context"), "tensor"),
        P("tensor"),
        P("tensor"),
        P("tensor"),
        P(None, "tensor"),
        P("tensor"),
        P("tensor"),
        P("tensor", None),
        P(("dp", "context"), "tensor"),
        P(),
        P("context", "tensor"),
        P("context", "tensor"),
        P("context", "tensor"),
        P(("dp", "context")),
        P(("dp", "context"), None),
    )
    out_specs = (P(("dp", "context"), "tensor"), P(("dp", "context"), "tensor"))
    return jax.shard_map(
        per_device, mesh=mesh, in_specs=in_specs, out_specs=out_specs, check_vma=False
    )
```

```python
import math

import jax
import jax.numpy as jnp
from jax import lax
from jax.experimental import pallas as pl
from jax.experimental.pallas import tpu as pltpu
from jax.sharding import PartitionSpec as P

P_SIZE = 64
NS = 128
HEAD_DIMENSION = 128
N_CTX = 32
N_Y = 4
N_Z = 8
N_T = 4
WINDOW = 18
DOCS = 16

epsilon = 1e-05
rope_base = 500000.0
MESH = pl.DeviceIdType.MESH
VMEM = pltpu.VMEM
DMA = pltpu.SemaphoreType.DMA


def context_peer(index):
    return {"context": index}


def tensor_peer(index):
    return {"tensor": index}


def remote(src, dst, send_sem, recv_sem, peer):
    return pltpu.make_async_remote_copy(
        src_ref=src,
        dst_ref=dst,
        send_sem=send_sem,
        recv_sem=recv_sem,
        device_id=peer,
        device_id_type=MESH,
    )


def barrier_context(me):
    barrier = pltpu.get_barrier_semaphore()

    def signal(step, carry):
        pl.semaphore_signal(
            barrier,
            inc=1,
            device_id=context_peer(lax.rem(me + step, N_CTX)),
            device_id_type=MESH,
        )
        return carry

    lax.fori_loop(1, N_CTX, signal, 0)
    return barrier


def softplus(value):
    return jnp.maximum(value, 0.0) + jnp.log1p(jnp.exp(-jnp.abs(value)))


def ssm_kernel(
    mixer,
    before,
    marks,
    docs_row,
    docs_tile,
    gate,
    dt,
    dt_turned,
    bias,
    bias_turned,
    rate,
    rate_turned,
    skip,
    taps,
    conv_bias,
    gain,
    shard,
    normed_ref,
    side_out,
    shards_ref,
    extended,
    conv,
    side,
    pieces,
    recv,
    scanned,
    incoming,
    base,
    send1,
    recv1,
    send2,
    recv2,
    send3,
    recv3,
    up_send,
    up_recv,
    down_send,
    down_recv,
):
    me = lax.axis_index("context")
    core = lax.axis_index("dp")
    row = lax.div(me, N_Z)
    col = lax.rem(me, N_Z)
    above = context_peer(row * N_Z + lax.rem(col + 1, N_Z))
    below = context_peer(row * N_Z + lax.rem(col + N_Z - 1, N_Z))
    barrier = barrier_context(me)
    rows = mixer.shape[0]
    channels = mixer.shape[1]
    heads = dt.shape[1]
    width = heads * P_SIZE
    pad = before.shape[0]
    lag = taps.shape[0] - 1
    pairs = width // NS
    exact = lax.Precision.HIGHEST

    extended[:pad] = before[:, :channels].astype(jnp.float32)
    extended[pad:] = mixer[...].astype(jnp.float32)
    running = conv_bias[...] + taps[lag : lag + 1] * extended[pad:]
    for offset in range(lag):
        begin = pad - lag + offset
        running = running + taps[offset : offset + 1] * (
            marks[:, 1 + offset : 2 + offset] * extended[begin : begin + rows]
        )
    conv[...] = (running * jax.nn.sigmoid(running)).astype(jnp.bfloat16)
    in_b = conv[:, width : width + NS]
    out_c = conv[:, width + NS :]

    first = lax.broadcasted_iota(jnp.int32, (rows, rows), 0)
    second = lax.broadcasted_iota(jnp.int32, (rows, rows), 1)
    step = softplus(dt[...] + bias[...])
    cumul = jnp.dot(
        jnp.where(first >= second, 1.0, 0.0),
        -step * jnp.exp(rate[...]),
        precision=exact,
        preferred_element_type=jnp.float32,
    )
    step_turned = softplus(dt_turned[...] + bias_turned[...])
    cumul_turned = jnp.dot(
        -step_turned * jnp.exp(rate_turned[...]),
        jnp.where(first <= second, 1.0, 0.0),
        precision=exact,
        preferred_element_type=jnp.float32,
    )
    carry_on = marks[:, 4:5]
    end_weight = jnp.exp(cumul[rows - 1 : rows] - cumul) * marks[:, 5:6] * step
    begin_weight = jnp.exp(cumul) * carry_on
    through = jnp.exp(cumul_turned[:, rows - 1 : rows]) * marks[rows - 1 : rows, 4:5]
    lower = lax.broadcasted_iota(jnp.int32, (rows, NS), 1) < P_SIZE

    def spread(value, pair):
        return jnp.where(
            lower, value[:, 2 * pair : 2 * pair + 1], value[:, 2 * pair + 1 : 2 * pair + 2]
        )

    each = N_CTX // pairs
    for pair in range(pairs):
        lanes = slice(pair * NS, (pair + 1) * NS)
        scaled = (conv[:, lanes].astype(jnp.float32) * spread(end_weight, pair)).astype(
            jnp.bfloat16
        )
        state = lax.dot_general(
            scaled, in_b, (((0,), (0,)), ((), ())), preferred_element_type=jnp.float32
        )
        pieces[pair * each : (pair + 1) * each] = state.reshape(
            each, NS // each, NS
        ).astype(jnp.bfloat16)
    docs_rows = docs_tile.shape[0]
    for head in range(heads):
        tile = jnp.concatenate(
            [
                docs_tile[...],
                jnp.broadcast_to(through[head : head + 1], (8 - docs_rows, NS)),
            ],
            axis=0,
        )
        for part in range(N_CTX // heads):
            side[head * (N_CTX // heads) + part] = tile

    def piece_copy(target, slot, number):
        return remote(
            pieces.at[target], recv.at[slot], send1.at[number], recv1.at[slot], context_peer(target)
        )

    def side_copy(target, slot, number):
        return remote(
            side.at[target], side_out.at[slot], send2.at[number], recv2.at[slot], context_peer(target)
        )

    def back_copy(target, slot, number):
        return remote(
            scanned.at[target],
            incoming.at[slot],
            send3.at[number],
            recv3.at[slot],
            context_peer(target),
        )

    def shard_up(distance):
        place = lax.rem(col + N_Z - distance, N_Z)
        return remote(
            shard.at[core] if distance == 0 else shards_ref.at[place],
            shards_ref.at[place],
            up_send.at[distance],
            up_recv.at[distance],
            above,
        )

    def shard_down(distance):
        place = lax.rem(col + distance, N_Z)
        return remote(
            shard.at[core] if distance == 0 else shards_ref.at[place],
            shards_ref.at[place],
            down_send.at[distance],
            down_recv.at[distance],
            below,
        )

    pl.semaphore_wait(barrier, N_CTX - 1)

    def start_out(number, carry):
        target = lax.rem(me + number, N_CTX)
        side_copy(target, me, number).start()
        piece_copy(target, me, number).start()
        return carry

    lax.fori_loop(1, N_CTX, start_out, 0)
    shard_up(0).start()
    shard_down(0).start()
    recv[me] = pieces[me]
    side_out[me] = side[me]
    shards_ref[col] = shard[core]

    mixing = lax.dot_general(
        out_c, in_b, (((1,), (1,)), ((), ())), preferred_element_type=jnp.float32
    )
    mixing = jnp.where((first >= second) & (marks[:, 0:1] == docs_row[...]), mixing, 0.0)
    for pair in range(pairs):
        lanes = slice(pair * NS, (pair + 1) * NS)
        inputs = conv[:, lanes]
        results = []
        for head in (2 * pair, 2 * pair + 1):
            fall = jnp.minimum(
                cumul[:, head : head + 1] - cumul_turned[head : head + 1], 0.0
            )
            weight = jnp.exp(fall) * mixing * step_turned[head : head + 1]
            results.append(
                jnp.dot(
                    weight.astype(jnp.bfloat16), inputs, preferred_element_type=jnp.float32
                )
            )
        base[:, lanes] = jnp.where(lower, results[0], results[1]) + skip[
            :, lanes
        ] * inputs.astype(jnp.float32)

    def arrive(number, carry):
        source = lax.rem(me + number, N_CTX)
        side_copy(source, source, number).wait_recv()
        piece_copy(source, source, number).wait_recv()
        return carry

    lax.fori_loop(1, N_CTX, arrive, 0)

    def one(turn, state):
        scanned[turn] = state.astype(jnp.bfloat16)
        return state * side_out[turn, docs_rows : docs_rows + 1, :] + recv[turn].astype(
            jnp.float32
        )

    lax.fori_loop(0, N_CTX, one, jnp.zeros(recv.shape[1:], jnp.float32))
    incoming[me] = scanned[me]

    def start_back(number, carry):
        back_copy(lax.rem(me + number, N_CTX), me, number).start()
        return carry

    lax.fori_loop(1, N_CTX, start_back, 0)

    def shard_turn(distance):
        shard_up(distance - 1).wait_recv()
        shard_up(distance).start()
        if distance < 3:
            shard_down(distance - 1).wait_recv()
            shard_down(distance).start()

    shard_turn(1)
    gated_by = gate[...].astype(jnp.float32)
    gated_by = gated_by * jax.nn.sigmoid(gated_by)
    shard_turn(2)

    def returned(number, carry):
        source = lax.rem(me + number, N_CTX)
        back_copy(source, source, number).wait_recv()
        return carry

    lax.fori_loop(1, N_CTX, returned, 0)
    shard_turn(3)
    squares = jnp.zeros((rows, 1), jnp.float32)
    for pair in range(pairs):
        lanes = slice(pair * NS, (pair + 1) * NS)
        carried = incoming[pair * each : (pair + 1) * each].reshape(NS, NS)
        arrived = lax.dot_general(
            out_c, carried, (((1,), (1,)), ((), ())), preferred_element_type=jnp.float32
        )
        gated = (base[:, lanes] + spread(begin_weight, pair) * arrived) * gated_by[:, lanes]
        base[:, lanes] = gated
        squares = squares + jnp.sum(gated * gated, axis=1, keepdims=True)
    scale = lax.rsqrt(squares / width + epsilon)
    normed_ref[...] = (base[...] * scale * gain[...]).astype(jnp.bfloat16)

    shard_down(2).wait_recv()
    shard_up(3).wait_recv()

    def finish(number, carry):
        source = lax.rem(me + number, N_CTX)
        piece_copy(source, source, number).wait_send()
        side_copy(source, source, number).wait_send()
        back_copy(source, source, number).wait_send()
        return carry

    lax.fori_loop(1, N_CTX, finish, 0)
    for distance in range(4):
        shard_up(distance).wait_send()
        if distance < 3:
            shard_down(distance).wait_send()


def mix(*operands):
    mixer, dt, shard = operands[0], operands[6], operands[16]
    rows, channels = mixer.shape
    width = dt.shape[1] * P_SIZE
    shape = (N_CTX, width // N_CTX, NS)
    spec = pl.BlockSpec(memory_space=VMEM)
    return pl.pallas_call(
        ssm_kernel,
        out_shape=(
            jax.ShapeDtypeStruct((rows, width), jnp.bfloat16),
            jax.ShapeDtypeStruct((N_CTX, 8, NS), jnp.float32),
            jax.ShapeDtypeStruct((N_Z,) + shard.shape[1:], jnp.bfloat16),
        ),
        in_specs=[spec] * len(operands),
        out_specs=(spec, spec, spec),
        scratch_shapes=[
            VMEM((rows + 8, channels), jnp.float32),
            VMEM((rows, channels), jnp.bfloat16),
            VMEM((N_CTX, 8, NS), jnp.float32),
            VMEM(shape, jnp.bfloat16),
            VMEM(shape, jnp.bfloat16),
            VMEM(shape, jnp.bfloat16),
            VMEM(shape, jnp.bfloat16),
            VMEM((rows, width), jnp.float32),
        ]
        + [DMA((N_CTX,))] * 6
        + [DMA((4,))] * 4,
        compiler_params=pltpu.CompilerParams(
            collective_id=0, has_side_effects=True, vmem_limit_bytes=48 * 1024 * 1024
        ),
        name="mix",
    )(*operands)


def project_kernel(
    normed,
    w_out,
    residual,
    gain,
    weights,
    cosine,
    sine,
    hidden_ref,
    query_ref,
    pair_ref,
    w_tiles,
    relay_a,
    relay_b,
    accum_a,
    accum_b,
    direct_a,
    direct_b,
    stage,
    hold_a,
    hold_b,
    full,
    gathered,
    load_sem,
    rs_send,
    rs_recv,
    ag_send,
    ag_recv,
    y_send,
    y_recv,
    core_send,
    core_recv,
):
    me = lax.axis_index("tensor")
    place = lax.axis_index("context")
    core = lax.axis_index("dp")
    other = 1 - core
    right = lax.rem(me + 1, N_T)
    left = lax.rem(me + 3, N_T)
    opposite = lax.rem(me + 2, N_T)
    row = lax.div(place, N_Z)
    col = lax.rem(place, N_Z)
    up = lax.rem(row + 1, N_Y)
    down = lax.rem(row + 3, N_Y)
    far = lax.rem(row + 2, N_Y)
    half = normed.shape[0] // 2
    width = residual.shape[1]

    barrier = pltpu.get_barrier_semaphore()
    for peer in (
        tensor_peer(right),
        tensor_peer(left),
        context_peer(up * N_Z + col),
        context_peer(down * N_Z + col),
        {"dp": other},
    ):
        pl.semaphore_signal(barrier, inc=1, device_id=peer, device_id_type=MESH)
    order = (opposite, right, left, me)

    def tile_load(number):
        column = pl.multiple_of(order[number] * width, width)
        return pltpu.make_async_copy(
            w_out.at[:, pl.ds(column, width)], w_tiles.at[number], load_sem.at[number]
        )

    for number in range(N_T):
        tile_load(number).start()
    gathered[pl.ds(row * N_Z, N_Z), core] = weights[...]

    def multiply(number):
        tile_load(number).wait()
        return jnp.dot(normed[...], w_tiles[number], preferred_element_type=jnp.float32)

    product = multiply(0)
    stage[0] = product[:half].astype(jnp.bfloat16)
    stage[1] = product[half:].astype(jnp.bfloat16)

    pl.semaphore_wait(barrier, 5)

    rs = [
        remote(stage.at[0], relay_a, rs_send.at[0], rs_recv.at[0], tensor_peer(right)),
        remote(stage.at[1], relay_b, rs_send.at[1], rs_recv.at[1], tensor_peer(left)),
        remote(stage.at[2], direct_b, rs_send.at[2], rs_recv.at[2], tensor_peer(right)),
        remote(stage.at[3], direct_a, rs_send.at[3], rs_recv.at[3], tensor_peer(left)),
        remote(stage.at[4], accum_a, rs_send.at[4], rs_recv.at[4], tensor_peer(right)),
        remote(stage.at[5], accum_b, rs_send.at[5], rs_recv.at[5], tensor_peer(left)),
    ]
    rs[0].start()
    rs[1].start()

    def row_copy(owner_row, begin, count, number, target_row):
        return remote(
            weights if number < 2 else gathered.at[pl.ds(owner_row * N_Z + begin, count), core],
            gathered.at[pl.ds(owner_row * N_Z + begin, count), core],
            y_send.at[number],
            y_recv.at[number],
            context_peer(target_row * N_Z + col),
        )

    quarter = N_Z // 2
    row_copy(row, 0, N_Z, 0, up).start()
    row_copy(row, 0, N_Z, 1, down).start()

    def core_copy(owner_row, number, source=None):
        return remote(
            gathered.at[pl.ds(owner_row * N_Z, N_Z), core] if source is None else source,
            gathered.at[pl.ds(owner_row * N_Z, N_Z), core],
            core_send.at[number],
            core_recv.at[number],
            {"dp": other},
        )

    def core_arrival(owner_row, number):
        return remote(
            gathered.at[pl.ds(owner_row * N_Z, N_Z), other],
            gathered.at[pl.ds(owner_row * N_Z, N_Z), other],
            core_send.at[number],
            core_recv.at[number],
            {"dp": other},
        )

    core_copy(row, 0, weights).start()

    product = multiply(1)
    stage[2] = product[half:].astype(jnp.bfloat16)
    hold_a[...] = product[:half]
    rs[2].start()
    product = multiply(2)
    stage[3] = product[:half].astype(jnp.bfloat16)
    hold_b[...] = product[half:]
    rs[3].start()
    rs[0].wait_recv()
    stage[4] = (hold_a[...] + relay_a[...].astype(jnp.float32)).astype(jnp.bfloat16)
    rs[4].start()
    rs[1].wait_recv()
    stage[5] = (hold_b[...] + relay_b[...].astype(jnp.float32)).astype(jnp.bfloat16)
    rs[5].start()
    product = multiply(3)
    hold_a[...] = product[:half]
    hold_b[...] = product[half:]
    rs[3].wait_recv()
    rs[4].wait_recv()
    hidden_a = (
        residual[:half].astype(jnp.float32)
        + (
            hold_a[...]
            + (direct_a[...].astype(jnp.float32) + accum_a[...].astype(jnp.float32))
        )
    ).astype(jnp.bfloat16)
    full[me, 0] = hidden_a
    hidden_ref[:half] = hidden_a
    rs[2].wait_recv()
    rs[5].wait_recv()
    hidden_b = (
        residual[half:].astype(jnp.float32)
        + (
            hold_b[...]
            + (direct_b[...].astype(jnp.float32) + accum_b[...].astype(jnp.float32))
        )
    ).astype(jnp.bfloat16)
    full[me, 1] = hidden_b
    hidden_ref[half:] = hidden_b

    def full_copy(owner, part, number, target):
        return remote(
            full.at[owner, part],
            full.at[owner, part],
            ag_send.at[number],
            ag_recv.at[number],
            tensor_peer(target),
        )

    full_copy(me, 0, 0, right).start()
    full_copy(me, 1, 3, left).start()
    full_copy(me, 1, 1, right).start()
    full_copy(me, 0, 2, left).start()

    full_copy(left, 0, 0, right).wait_recv()
    full_copy(left, 0, 4, right).start()
    full_copy(right, 1, 3, left).wait_recv()
    full_copy(right, 1, 5, left).start()

    row_copy(down, 0, N_Z, 0, up).wait_recv()
    row_copy(down, 0, quarter, 2, up).start()
    core_copy(down, 1).start()
    row_copy(up, 0, N_Z, 1, down).wait_recv()
    row_copy(up, quarter, quarter, 3, down).start()
    core_copy(up, 2).start()

    full_copy(left, 1, 1, right).wait_recv()
    full_copy(right, 0, 2, left).wait_recv()
    full_copy(opposite, 0, 4, right).wait_recv()
    full_copy(opposite, 1, 5, left).wait_recv()

    row_copy(far, 0, quarter, 2, up).wait_recv()
    row_copy(far, quarter, quarter, 3, down).wait_recv()
    core_copy(far, 3).start()

    core_arrival(row, 0).wait_recv()
    core_arrival(down, 1).wait_recv()
    core_arrival(up, 2).wait_recv()
    core_arrival(far, 3).wait_recv()

    rows_each = gathered.shape[0] // N_T
    depth = rows_each * gathered.shape[1] * gathered.shape[2]
    for part in range(2):
        squares = jnp.zeros((half, 1), jnp.float32)
        for owner in range(N_T):
            stream = full[owner, part].astype(jnp.float32)
            squares = squares + jnp.sum(stream * stream, axis=1, keepdims=True)
        scale = lax.rsqrt(squares / (N_T * width) + epsilon)
        total = jnp.zeros((half, weights.shape[2]), jnp.float32)
        for owner in range(N_T):
            stream = full[owner, part].astype(jnp.float32)
            block = (stream * scale * gain[:, owner * width : (owner + 1) * width]).astype(
                jnp.bfloat16
            )
            piece = gathered[owner * rows_each : (owner + 1) * rows_each].reshape(
                depth, gathered.shape[3]
            )
            total = total + jnp.dot(block, piece, preferred_element_type=jnp.float32)
        rows = slice(part * half, (part + 1) * half)
        count = total.shape[1] // HEAD_DIMENSION
        for head in range(count):
            lanes = slice(head * HEAD_DIMENSION, (head + 1) * HEAD_DIMENSION)
            value = total[:, lanes]
            if head < count - 1:
                value = value * cosine[rows] + pltpu.roll(value, HEAD_DIMENSION // 2, 1) * sine[rows]
            if head < count - 2:
                begin = head * 2 * half + part * half
                query_ref[:, begin : begin + half] = value.T.astype(jnp.bfloat16)
            elif head < count - 1:
                pair_ref[0, rows] = value.astype(jnp.bfloat16)
            else:
                pair_ref[1, rows] = value.T.astype(jnp.bfloat16)

    for copy in rs:
        copy.wait_send()
    full_copy(me, 0, 0, right).wait_send()
    full_copy(me, 1, 3, left).wait_send()
    full_copy(me, 1, 1, right).wait_send()
    full_copy(me, 0, 2, left).wait_send()
    full_copy(left, 0, 4, right).wait_send()
    full_copy(right, 1, 5, left).wait_send()
    row_copy(row, 0, N_Z, 0, up).wait_send()
    row_copy(row, 0, N_Z, 1, down).wait_send()
    row_copy(down, 0, quarter, 2, up).wait_send()
    row_copy(up, quarter, quarter, 3, down).wait_send()
    core_copy(row, 0).wait_send()
    core_copy(down, 1).wait_send()
    core_copy(up, 2).wait_send()
    core_copy(far, 3).wait_send()


def project(normed, w_out, residual, gain, weights, cosine, sine):
    rows, width = residual.shape
    half = rows // 2
    out_width = weights.shape[2]
    spec = pl.BlockSpec(memory_space=VMEM)
    piece = VMEM((half, width), jnp.bfloat16)
    return pl.pallas_call(
        project_kernel,
        out_shape=(
            jax.ShapeDtypeStruct((rows, width), jnp.bfloat16),
            jax.ShapeDtypeStruct(
                (HEAD_DIMENSION, rows * (out_width // HEAD_DIMENSION - 2)), jnp.bfloat16
            ),
            jax.ShapeDtypeStruct((2, rows, HEAD_DIMENSION), jnp.bfloat16),
        ),
        in_specs=[spec, pl.BlockSpec(memory_space=pl.ANY)] + [spec] * 5,
        out_specs=(spec, spec, spec),
        scratch_shapes=[
            VMEM((N_T, width, width), jnp.bfloat16),
            piece,
            piece,
            piece,
            piece,
            piece,
            piece,
            VMEM((6, half, width), jnp.bfloat16),
            VMEM((half, width), jnp.float32),
            VMEM((half, width), jnp.float32),
            VMEM((N_T, 2, half, width), jnp.bfloat16),
            VMEM((N_CTX, 2) + weights.shape[1:], jnp.bfloat16),
            DMA((N_T,)),
            DMA((6,)),
            DMA((6,)),
            DMA((6,)),
            DMA((6,)),
            DMA((4,)),
            DMA((4,)),
            DMA((4,)),
            DMA((4,)),
        ],
        compiler_params=pltpu.CompilerParams(
            collective_id=1, has_side_effects=True, vmem_limit_bytes=56 * 1024 * 1024
        ),
        name="project",
    )(normed, w_out, residual, gain, weights, cosine, sine)


def attend_kernel(
    chosen,
    queries,
    keys_values,
    starts,
    out_ref,
    window,
    rows_buf,
    outgoing,
    best_ref,
    denom_ref,
    accum_ref,
    up_send,
    down_send,
    across_send,
    recv_sem,
    out_send,
    out_recv,
):
    me = lax.axis_index("context")
    barrier = barrier_context(me)
    window[0] = keys_values[...]
    number = queries.shape[1]
    tokens = keys_values.shape[1]
    group = number // tokens
    scale = HEAD_DIMENSION ** (-0.5) / math.log(2.0)

    def masked_scores(slot):
        keys = window[slot, 0]
        scores = scale * jnp.dot(keys, queries[...], preferred_element_type=jnp.float32)
        key_index = lax.broadcasted_iota(jnp.int32, (tokens, number), 0)
        usable = key_index >= starts[...] - tokens * (me - slot)
        return scores, usable, key_index

    def weighted(slot, probs):
        values = jnp.concatenate(
            [
                window[slot, 1, :HEAD_DIMENSION],
                window[slot, 1, HEAD_DIMENSION:],
            ],
            axis=1,
        )
        return jnp.dot(values, probs.astype(jnp.bfloat16), preferred_element_type=jnp.float32)

    def attend_first():
        scores, usable, key_index = masked_scores(0)
        query_index = lax.rem(lax.broadcasted_iota(jnp.int32, (1, number), 1), tokens)
        scores = jnp.where(usable & (key_index <= query_index), scores, -1e30)
        top = jnp.max(scores, axis=0, keepdims=True)
        probs = jnp.exp2(scores - top)
        best_ref[...] = top
        denom_ref[...] = jnp.sum(probs, axis=0, keepdims=True)
        accum_ref[...] = weighted(0, probs)

    def attend(slot):
        scores, usable, _ = masked_scores(slot)
        scores = jnp.where(usable, scores, -1e30)
        before = best_ref[...]
        fresh = jnp.maximum(before, jnp.max(scores, axis=0, keepdims=True))
        fade = jnp.exp2(before - fresh)
        probs = jnp.exp2(scores - fresh)
        best_ref[...] = fresh
        denom_ref[...] = denom_ref[...] * fade + jnp.sum(probs, axis=0, keepdims=True)
        accum_ref[...] = accum_ref[...] * fade + weighted(slot, probs)

    row = lax.div(me, N_Z)
    col = lax.rem(me, N_Z)
    inner = col < N_Z - 1
    forward = row * N_Z + lax.rem(col + 1, N_Z)
    backward = lax.rem(me + N_CTX - 1, N_CTX)
    across = lax.rem(me + N_Z, N_CTX)
    up_base = jnp.where(inner, 0, N_Z)
    up_shift = jnp.where(inner, 1, 1 - N_Z)

    def send_up(slot, part):
        return remote(
            window.at[slot, part],
            window.at[slot + up_shift, part],
            up_send.at[slot, part],
            recv_sem.at[slot + up_shift, part],
            context_peer(forward),
        )

    def send_down(slot, part):
        return remote(
            window.at[slot, part],
            window.at[slot - 1, part],
            down_send.at[slot, part],
            recv_sem.at[slot - 1, part],
            context_peer(backward),
        )

    def send_across(slot, part):
        return remote(
            window.at[slot, part],
            window.at[slot + N_Z, part],
            across_send.at[slot, part],
            recv_sem.at[slot + N_Z, part],
            context_peer(across),
        )

    attend_first()
    pl.semaphore_wait(barrier, N_CTX - 1)
    for part in range(2):
        send_across(0, part).start()

        @pl.when(inner)
        def _():
            send_up(0, part).start()

    visits = (8, 1, 7, 16, 9, 2, 6, 15, 10, 3, 14, 5, 17, 11, 13, 4, 12)
    goes_down = (6, 7, 8, 13, 14, 15, 16)
    goes_across = (1, 2, 3, 8, 9)

    def visit(step, carry):
        slot = jnp.int32(visits[0])
        for number_here, value in enumerate(visits):
            slot = jnp.where(step == number_here, value, slot)
        upward = (slot >= up_base) & (slot <= up_base + 3)
        downward = ((slot >= 6) & (slot <= 8)) | ((slot >= 13) & (slot <= 16))
        crossing = (slot <= 3) | (slot == 8) | (slot == 9)
        for part in range(2):
            remote(
                window.at[slot, part],
                window.at[slot, part],
                down_send.at[slot, part],
                recv_sem.at[slot, part],
                context_peer(forward),
            ).wait_recv()

            @pl.when(crossing)
            def _():
                send_across(slot, part).start()

            @pl.when(upward)
            def _():
                send_up(slot, part).start()

            @pl.when(downward)
            def _():
                send_down(slot, part).start()

        attend(slot)
        return carry

    lax.fori_loop(0, len(visits), visit, 0)

    result = accum_ref[...] / denom_ref[...]
    for head in range(group):
        lanes = slice(head * HEAD_DIMENSION, (head + 1) * HEAD_DIMENSION)
        rows_buf[:, :, lanes] = (
            result[:, head * tokens : (head + 1) * tokens]
            .T.reshape(N_CTX, tokens // N_CTX, HEAD_DIMENSION)
            .astype(jnp.bfloat16)
        )

    def place_row(index, carry):
        outgoing[index] = rows_buf[chosen[index]]
        return carry

    lax.fori_loop(0, N_CTX, place_row, 0)
    out_ref[me] = outgoing[me]

    def row_copy(target, slot, step):
        return remote(
            outgoing.at[target],
            out_ref.at[slot],
            out_send.at[step],
            out_recv.at[slot],
            context_peer(target),
        )

    def start_rows(step, carry):
        row_copy(lax.rem(me + step, N_CTX), me, step).start()
        return carry

    lax.fori_loop(1, N_CTX, start_rows, 0)
    for part in range(2):
        for slot in range(4):
            send_up(slot + up_base, part).wait_send()
        for slot in goes_down:
            send_down(slot, part).wait_send()
        for slot in (0,) + goes_across:
            send_across(slot, part).wait_send()

    def finish(step, carry):
        source = lax.rem(me + step, N_CTX)
        row_copy(source, source, step).wait_recv()
        row_copy(source, source, step).wait_send()
        return carry

    lax.fori_loop(1, N_CTX, finish, 0)


def attend(chosen, queries, keys_values, starts):
    number = queries.shape[1]
    _, tokens, depth = keys_values.shape
    out_width = number // tokens * HEAD_DIMENSION
    spec = pl.BlockSpec(memory_space=VMEM)
    rows = (N_CTX, tokens // N_CTX, out_width)
    return pl.pallas_call(
        attend_kernel,
        out_shape=jax.ShapeDtypeStruct(rows, jnp.bfloat16),
        in_specs=[pl.BlockSpec(memory_space=pltpu.SMEM)] + [spec] * 3,
        out_specs=spec,
        scratch_shapes=[
            VMEM((WINDOW, 2, tokens, depth), jnp.bfloat16),
            VMEM(rows, jnp.bfloat16),
            VMEM(rows, jnp.bfloat16),
            VMEM((1, number), jnp.float32),
            VMEM((1, number), jnp.float32),
            VMEM((HEAD_DIMENSION, number), jnp.float32),
            DMA((WINDOW, 2)),
            DMA((WINDOW, 2)),
            DMA((WINDOW, 2)),
            DMA((WINDOW, 2)),
            DMA((N_CTX,)),
            DMA((N_CTX,)),
        ],
        compiler_params=pltpu.CompilerParams(
            collective_id=2, has_side_effects=True, vmem_limit_bytes=48 * 1024 * 1024
        ),
        name="attend",
    )(chosen, queries, keys_values, starts)


def per_device(
    mixer_input,
    gate_z,
    dt_raw,
    dt_bias,
    a_log,
    d_skip,
    conv_weight,
    conv_bias,
    norm_gain,
    w_out,
    residual,
    attn_gain,
    w_query,
    w_key,
    value_weight,
    doc_ids,
    owners,
):
    row_count = mixer_input.shape[0]
    position_here = lax.axis_index("context")
    first_row = position_here * row_count
    lag = conv_weight.shape[0] - 1
    channels = mixer_input.shape[1]
    halo = 8
    last_rows = jnp.concatenate(
        [
            mixer_input[row_count - halo :],
            jnp.broadcast_to(
                doc_ids[row_count - halo :, None].astype(jnp.bfloat16), (halo, HEAD_DIMENSION)
            ),
        ],
        axis=1,
    )
    before = lax.ppermute(
        last_rows, "context", [(source, source + 1) for source in range(N_CTX - 1)]
    )
    docs = doc_ids.astype(jnp.float32)
    before_docs = jnp.where(
        position_here > 0, before[halo - lag :, channels].astype(jnp.float32), -1.0
    )
    extended_docs = jnp.concatenate([before_docs, docs])
    marks = jnp.stack(
        [docs]
        + [
            (extended_docs[offset : offset + row_count] == docs).astype(jnp.float32)
            for offset in range(lag)
        ]
        + [
            (docs == before_docs[lag - 1]).astype(jnp.float32),
            (docs == docs[row_count - 1]).astype(jnp.float32),
        ],
        axis=1,
    )
    shard = jnp.concatenate([w_query, w_key, value_weight], axis=1)
    shard = shard.reshape(2, shard.shape[0] // 2, shard.shape[1])
    docs_tile = docs.reshape(row_count // NS, NS)
    normed_ssm, side_all, shards = mix(
        mixer_input,
        before,
        marks,
        docs[None, :],
        docs_tile,
        gate_z,
        dt_raw,
        dt_raw.T,
        dt_bias[None, :],
        dt_bias[:, None],
        a_log[None, :],
        a_log[:, None],
        jnp.repeat(d_skip, P_SIZE)[None, :],
        conv_weight,
        conv_bias[None, :],
        norm_gain[None, :],
        shard,
    )
    all_docs = side_all[:, : docs_tile.shape[0]].reshape(N_CTX, row_count)

    positions = first_row + jnp.arange(row_count, dtype=jnp.int32)
    half_width = HEAD_DIMENSION // 2
    freqs = jnp.exp(
        jnp.arange(half_width, dtype=jnp.float32) * (-2.0 * math.log(rope_base) / HEAD_DIMENSION)
    )
    angles = positions.astype(jnp.float32)[:, None] * freqs[None, :]
    cosine = jnp.cos(angles)
    sine = jnp.sin(angles)
    cosine = jnp.concatenate([cosine, cosine], axis=1)
    sine = jnp.concatenate([-sine, sine], axis=1)
    hidden_out, queries, keys_values = project(
        normed_ssm, w_out, residual, attn_gain[None, :], shards, cosine, sine
    )
    query_width = w_query.shape[1]
    group = query_width // HEAD_DIMENSION
    device_ids = jnp.arange(N_CTX, dtype=jnp.int32)
    chosen = jnp.sum(
        jnp.where(owners[0][None, :] == device_ids[:, None], device_ids[None, :], 0), axis=1
    )
    names = jnp.arange(DOCS, dtype=jnp.int32).astype(jnp.float32)
    doc_starts = jnp.sum(
        (all_docs.reshape(1, -1) < names[:, None]).astype(jnp.int32), axis=1
    )
    starts = jnp.sum(
        jnp.where(
            doc_ids.astype(jnp.float32)[None, :] == names[:, None], doc_starts[:, None], 0
        ),
        axis=0,
    )
    attended = attend(chosen, queries, keys_values, jnp.tile(starts, group)[None, :])
    return (hidden_out, attended.reshape(row_count, query_width))


def solution(mesh):
    in_specs = (
        P(("dp", "context"), "tensor"),
        P(("dp", "context"), "tensor"),
        P(("dp", "context"), "tensor"),
        P("tensor"),
        P("tensor"),
        P("tensor"),
        P(None, "tensor"),
        P("tensor"),
        P("tensor"),
        P("tensor", None),
        P(("dp", "context"), "tensor"),
        P(),
        P("context", "tensor"),
        P("context", "tensor"),
        P("context", "tensor"),
        P(("dp", "context")),
        P(("dp", "context"), None),
    )
    out_specs = (P(("dp", "context"), "tensor"), P(("dp", "context"), "tensor"))
    return jax.shard_map(
        per_device, mesh=mesh, in_specs=in_specs, out_specs=out_specs, check_vma=False
    )
```

```python
import math
from types import SimpleNamespace

import jax
import jax.numpy as jnp
from jax import lax
from jax.experimental import pallas as pl
from jax.experimental.pallas import tpu as pltpu
from jax.sharding import PartitionSpec as P

P_SIZE = 64
NS = 128
HEAD_DIMENSION = 128
N_CTX = 32
N_Y = 4
N_Z = 8
N_T = 4
WINDOW = 18
DOCS = 16

epsilon = 1e-05
rope_base = 500000.0
MESH = pl.DeviceIdType.MESH
VMEM = pltpu.VMEM
DMA = pltpu.SemaphoreType.DMA


def context_peer(index):
    return {"context": index}


def tensor_peer(index):
    return {"tensor": index}


def remote(src, dst, send_sem, recv_sem, peer):
    return pltpu.make_async_remote_copy(
        src_ref=src,
        dst_ref=dst,
        send_sem=send_sem,
        recv_sem=recv_sem,
        device_id=peer,
        device_id_type=MESH,
    )


def softplus(value):
    return jnp.maximum(value, 0.0) + jnp.log1p(jnp.exp(-jnp.abs(value)))


def around(first, count, step, carry=None):
    lax.fori_loop(first, count, lambda number, none: (step(number), none)[1], 0)


def mix_phase(r, me, core):
    row = lax.div(me, N_Z)
    col = lax.rem(me, N_Z)
    above = context_peer(row * N_Z + lax.rem(col + 1, N_Z))
    below = context_peer(row * N_Z + lax.rem(col + N_Z - 1, N_Z))
    rows, channels = r.mixer.shape
    heads = r.dt.shape[0]
    width = heads * P_SIZE
    pairs = width // NS
    exact = lax.Precision.HIGHEST
    pad = 8
    edge = 16

    r.load_docs.wait()
    r.docs[...] = r.docs_raw[...].astype(jnp.float32)
    docs_row = jnp.concatenate([r.docs[0:1], r.docs[1:2]], axis=1)
    first = lax.broadcasted_iota(jnp.int32, (rows, rows), 0)
    second = lax.broadcasted_iota(jnp.int32, (rows, rows), 1)
    unit = jnp.where(first == second, 1.0, 0.0)
    nt = (((1,), (1,)), ((), ()))

    def turned(value, precision):
        return lax.dot_general(
            unit, value, nt, precision=precision, preferred_element_type=jnp.float32
        )

    docs_col = turned(jnp.broadcast_to(docs_row, (NS, rows)), exact)
    r.docs_ext[pad:] = docs_col

    r.load_taps.wait()
    r.load_conv_bias.wait()
    r.load_mixer.wait()
    r.extended[pad:] = r.mixer[...].astype(jnp.float32)

    def convolve(begin, count):
        here = r.docs_ext[pad + begin : pad + begin + count]
        masks = [
            jnp.where(
                r.docs_ext[pad - 3 + k + begin : pad - 3 + k + begin + count] == here, 1.0, 0.0
            )
            for k in range(3)
        ]
        for chunk in range(channels // NS):
            lanes = slice(chunk * NS, (chunk + 1) * NS)
            running = r.conv_bias[chunk : chunk + 1] + r.taps[3:4, lanes] * (
                r.extended[pad + begin : pad + begin + count, lanes]
            )
            for k in range(3):
                start = pad - 3 + k + begin
                running = running + r.taps[k : k + 1, lanes] * (
                    masks[k] * r.extended[start : start + count, lanes]
                )
            r.conv[begin : begin + count, lanes] = (running * jax.nn.sigmoid(running)).astype(
                jnp.bfloat16
            )

    convolve(edge, rows - edge)

    r.load_dt.wait()
    for small in r.load_small:
        small.wait()
    diagonal = lax.broadcasted_iota(jnp.int32, (heads, heads), 0) == lax.broadcasted_iota(
        jnp.int32, (heads, heads), 1
    )

    def column(ref):
        return jnp.sum(jnp.where(diagonal, ref[...], 0.0), axis=1, keepdims=True)

    bias, rate, skip = column(r.dt_bias), column(r.a_log), column(r.d_skip)
    step_turned = softplus(r.dt[...] + bias)
    cumul_turned = jnp.dot(
        -step_turned * jnp.exp(rate),
        jnp.where(first <= second, 1.0, 0.0),
        precision=exact,
        preferred_element_type=jnp.float32,
    )
    last_doc = docs_row[:, rows - 1 : rows]
    end_turned = (
        jnp.exp(cumul_turned[:, rows - 1 : rows] - cumul_turned)
        * jnp.where(docs_row == last_doc, 1.0, 0.0)
        * step_turned
    )
    cumul = turned(cumul_turned, exact)
    end_weight = turned(end_turned, exact)
    begin_weight = jnp.exp(cumul)
    lower = lax.broadcasted_iota(jnp.int32, (rows, NS), 1) < P_SIZE

    def spread(value, pair):
        return jnp.where(
            lower, value[:, 2 * pair : 2 * pair + 1], value[:, 2 * pair + 1 : 2 * pair + 2]
        )

    pl.semaphore_wait(pltpu.get_barrier_semaphore(), N_CTX - 1 + 3)

    following = context_peer(lax.rem(me + 1, N_CTX))
    halo_rows = remote(
        r.mixer.at[pl.ds(rows - edge, edge)], r.halo, r.halo_send.at[0], r.halo_recv.at[0], following
    )
    halo_docs = remote(
        r.docs_ext.at[pl.ds(rows, pad)],
        r.docs_ext.at[pl.ds(0, pad)],
        r.halo_send.at[1],
        r.halo_recv.at[1],
        following,
    )
    halo_docs.start()
    halo_rows.start()

    def docs_copy(target, slot, number):
        return remote(
            r.docs,
            r.docs_all.at[slot],
            r.docs_send.at[number],
            r.docs_recv.at[slot],
            context_peer(target),
        )

    for load in r.load_shard:
        load.wait()

    def shard_copy(place, distance, sends, recvs, target):
        return remote(
            r.shard if distance == 0 else r.shards.at[place],
            r.shards.at[place],
            sends.at[distance],
            recvs.at[distance],
            target,
        )

    def shard_up(distance):
        place = lax.rem(col + N_Z - distance, N_Z)
        return shard_copy(place, distance, r.up_send, r.up_recv, above)

    def shard_down(distance):
        place = lax.rem(col + distance, N_Z)
        return shard_copy(place, distance, r.down_send, r.down_recv, below)

    halo_docs.wait_recv()
    r.docs_ext[:pad] = jnp.where(me > 0, r.docs_ext[:pad], -1.0)
    halo_rows.wait_recv()
    r.extended[:pad] = r.halo[edge - pad :].astype(jnp.float32)
    convolve(0, edge)
    in_b = r.conv[:, width : width + NS]
    out_c = r.conv[:, width + NS :]
    prev_doc = r.docs_ext[pad - 1 : pad]
    carry_on = jnp.where(r.docs_ext[pad:] == prev_doc, 1.0, 0.0)
    through = jnp.exp(cumul_turned[:, rows - 1 : rows]) * jnp.where(
        last_doc == prev_doc[:, 0:1], 1.0, 0.0
    )

    each = N_CTX // pairs
    for pair in range(pairs):
        lanes = slice(pair * NS, (pair + 1) * NS)
        scaled = (r.conv[:, lanes].astype(jnp.float32) * spread(end_weight, pair)).astype(
            jnp.bfloat16
        )
        state = lax.dot_general(
            scaled, in_b, (((0,), (0,)), ((), ())), preferred_element_type=jnp.float32
        )
        r.pieces[pair * each : (pair + 1) * each] = state.reshape(
            each, NS // each, NS
        ).astype(jnp.bfloat16)
    for head in range(heads):
        for part in range(N_CTX // heads):
            r.side[head * (N_CTX // heads) + part] = jnp.broadcast_to(
                through[head : head + 1], (1, NS)
            )

    def piece_copy(target, slot, number):
        return remote(
            r.pieces.at[target],
            r.recv.at[slot],
            r.send1.at[number],
            r.recv1.at[slot],
            context_peer(target),
        )

    def side_copy(target, slot, number):
        return remote(
            r.side.at[target],
            r.side_all.at[slot],
            r.send2.at[number],
            r.recv2.at[slot],
            context_peer(target),
        )

    def back_copy(target, slot, number):
        return remote(
            r.scanned.at[target],
            r.incoming.at[slot],
            r.send3.at[number],
            r.recv3.at[slot],
            context_peer(target),
        )

    def start_out(number):
        target = lax.rem(me + number, N_CTX)
        side_copy(target, me, number).start()
        piece_copy(target, me, number).start()

    around(1, N_CTX, start_out)
    shard_up(0).start()
    shard_down(0).start()
    around(1, N_CTX, lambda number: docs_copy(lax.rem(me + number, N_CTX), me, number).start())
    r.docs_all[me] = r.docs[...]
    r.recv[me] = r.pieces[me]
    r.side_all[me] = r.side[me]
    r.shards[col] = r.shard[...]

    mixing = lax.dot_general(out_c, in_b, nt, preferred_element_type=jnp.float32)
    docs_wide = jnp.concatenate([docs_col, docs_col], axis=1)
    mixing = jnp.where((first >= second) & (docs_wide == docs_row), mixing, 0.0)
    for pair in range(pairs):
        lanes = slice(pair * NS, (pair + 1) * NS)
        inputs = r.conv[:, lanes]
        results = []
        for head in (2 * pair, 2 * pair + 1):
            fall = jnp.minimum(
                cumul[:, head : head + 1] - cumul_turned[head : head + 1], 0.0
            )
            weight = jnp.exp(fall) * mixing * step_turned[head : head + 1]
            results.append(
                jnp.dot(
                    weight.astype(jnp.bfloat16), inputs, preferred_element_type=jnp.float32
                )
            )
        r.base[:, lanes] = jnp.where(lower, results[0], results[1]) + jnp.where(
            lower[0:1], skip[2 * pair : 2 * pair + 1], skip[2 * pair + 1 : 2 * pair + 2]
        ) * inputs.astype(jnp.float32)

    def arrive(number):
        source = lax.rem(me + number, N_CTX)
        side_copy(source, source, number).wait_recv()
        piece_copy(source, source, number).wait_recv()

    around(1, N_CTX, arrive)

    def one(turn, state):
        r.scanned[turn] = state.astype(jnp.bfloat16)
        return state * r.side_all[turn] + r.recv[turn].astype(
            jnp.float32
        )

    lax.fori_loop(0, N_CTX, one, jnp.zeros(r.recv.shape[1:], jnp.float32))
    r.incoming[me] = r.scanned[me]

    def start_back(number):
        back_copy(lax.rem(me + number, N_CTX), me, number).start()

    around(1, N_CTX, start_back)

    def shard_turn(distance):
        shard_up(distance - 1).wait_recv()
        shard_up(distance).start()
        if distance < 3:
            shard_down(distance - 1).wait_recv()
            shard_down(distance).start()

    shard_turn(1)
    r.load_gate.wait()
    gated_by = r.gate[...].astype(jnp.float32)
    r.swish[...] = gated_by * jax.nn.sigmoid(gated_by)
    shard_turn(2)

    def returned(number):
        source = lax.rem(me + number, N_CTX)
        back_copy(source, source, number).wait_recv()

    around(1, N_CTX, returned)
    shard_turn(3)
    squares = jnp.zeros((rows, 1), jnp.float32)
    for pair in range(pairs):
        lanes = slice(pair * NS, (pair + 1) * NS)
        carried = r.incoming[pair * each : (pair + 1) * each].reshape(NS, NS)
        arrived = lax.dot_general(out_c, carried, nt, preferred_element_type=jnp.float32)
        gated = (
            r.base[:, lanes] + spread(begin_weight, pair) * carry_on * arrived
        ) * r.swish[:, lanes]
        r.base[:, lanes] = gated
        squares = squares + jnp.sum(gated * gated, axis=1, keepdims=True)
    scale = lax.rsqrt(squares / width + epsilon)
    r.load_gain.wait()
    r.normed[...] = (r.base[...] * scale * r.gain[...]).astype(jnp.bfloat16)

    def finish():
        def sent(number):
            source = lax.rem(me + number, N_CTX)
            piece_copy(source, source, number).wait_send()
            side_copy(source, source, number).wait_send()
            docs_copy(source, source, number).wait_send()
            back_copy(source, source, number).wait_send()

        around(1, N_CTX, sent)
        halo_rows.wait_send()
        halo_docs.wait_send()
        for distance in range(4):
            shard_up(distance).wait_send()
            if distance < 3:
                shard_down(distance).wait_send()

    def docs_arrive(number):
        source = lax.rem(me + number, N_CTX)
        docs_copy(source, source, number).wait_recv()

    def shards_arrive():
        shard_down(2).wait_recv()
        shard_up(3).wait_recv()
        around(1, N_CTX, docs_arrive)

    return finish, shards_arrive


def project_phase(r, me_context, core, shards_arrive):
    me = lax.axis_index("tensor")
    place = me_context
    other = 1 - core
    right = lax.rem(me + 1, N_T)
    left = lax.rem(me + 3, N_T)
    opposite = lax.rem(me + 2, N_T)
    row = lax.div(place, N_Z)
    col = lax.rem(place, N_Z)
    up = lax.rem(row + 1, N_Y)
    down = lax.rem(row + 3, N_Y)
    far = lax.rem(row + 2, N_Y)
    width = r.residual.shape[1]
    tokens = r.residual.shape[0]
    half = tokens // 2

    def multiply(number):
        r.load_tiles[number].wait()
        return jnp.dot(r.normed[...], r.w_tiles[number], preferred_element_type=jnp.float32)

    rs = [
        remote(r.stage.at[0], r.relay_a, r.rs_send.at[0], r.rs_recv.at[0], tensor_peer(right)),
        remote(r.stage.at[1], r.relay_b, r.rs_send.at[1], r.rs_recv.at[1], tensor_peer(left)),
        remote(r.stage.at[2], r.direct_b, r.rs_send.at[2], r.rs_recv.at[2], tensor_peer(right)),
        remote(r.stage.at[3], r.direct_a, r.rs_send.at[3], r.rs_recv.at[3], tensor_peer(left)),
        remote(r.stage.at[4], r.accum_a, r.rs_send.at[4], r.rs_recv.at[4], tensor_peer(right)),
        remote(r.stage.at[5], r.accum_b, r.rs_send.at[5], r.rs_recv.at[5], tensor_peer(left)),
    ]
    product = multiply(0)
    r.stage[0] = product[:half].astype(jnp.bfloat16)
    r.stage[1] = product[half:].astype(jnp.bfloat16)
    rs[0].start()
    rs[1].start()

    quarter = N_Z // 2

    def row_copy(owner_row, begin, count, number, target_row):
        part = r.gathered.at[pl.ds(owner_row * N_Z + begin, count), core]
        return remote(
            r.shards if number < 2 else part,
            part,
            r.y_send.at[number],
            r.y_recv.at[number],
            context_peer(target_row * N_Z + col),
        )

    def core_copy(owner_row, number, side=core, source=None):
        part = r.gathered.at[pl.ds(owner_row * N_Z, N_Z), side]
        return remote(
            part if source is None else source,
            part,
            r.core_send.at[number],
            r.core_recv.at[number],
            {"dp": other},
        )

    product = multiply(1)
    r.stage[2] = product[half:].astype(jnp.bfloat16)
    r.hold_a[...] = product[:half]
    rs[2].start()
    product = multiply(2)
    r.stage[3] = product[:half].astype(jnp.bfloat16)
    r.hold_b[...] = product[half:]
    rs[3].start()

    shards_arrive()
    row_copy(row, 0, N_Z, 0, up).start()
    row_copy(row, 0, N_Z, 1, down).start()
    core_copy(row, 0, core, r.shards).start()

    rs[0].wait_recv()
    r.stage[4] = (r.hold_a[...] + r.relay_a[...].astype(jnp.float32)).astype(jnp.bfloat16)
    rs[4].start()
    rs[1].wait_recv()
    r.stage[5] = (r.hold_b[...] + r.relay_b[...].astype(jnp.float32)).astype(jnp.bfloat16)
    rs[5].start()
    product = multiply(3)
    r.hold_a[...] = product[:half]
    r.hold_b[...] = product[half:]
    r.gathered[pl.ds(row * N_Z, N_Z), core] = r.shards[...]

    def full_copy(owner, part, number, target):
        return remote(
            r.full.at[owner, part],
            r.full.at[owner, part],
            r.ag_send.at[number],
            r.ag_recv.at[number],
            tensor_peer(target),
        )

    r.load_residual.wait()
    r.load_attn_gain.wait()
    rs[3].wait_recv()
    rs[4].wait_recv()
    r.full[me, 0] = (
        r.residual[:half].astype(jnp.float32)
        + (
            r.hold_a[...]
            + (r.direct_a[...].astype(jnp.float32) + r.accum_a[...].astype(jnp.float32))
        )
    ).astype(jnp.bfloat16)
    full_copy(me, 0, 0, right).start()
    full_copy(me, 0, 2, left).start()
    rs[2].wait_recv()
    rs[5].wait_recv()
    r.full[me, 1] = (
        r.residual[half:].astype(jnp.float32)
        + (
            r.hold_b[...]
            + (r.direct_b[...].astype(jnp.float32) + r.accum_b[...].astype(jnp.float32))
        )
    ).astype(jnp.bfloat16)
    full_copy(me, 1, 3, left).start()
    full_copy(me, 1, 1, right).start()
    hidden_out = pltpu.make_async_copy(r.full.at[me], r.hidden_ref, r.out_sem.at[0])
    hidden_out.start()

    lane = lax.broadcasted_iota(jnp.int32, (1, HEAD_DIMENSION), 1)
    pair = lax.rem(lane, HEAD_DIMENSION // 2).astype(jnp.float32)
    freqs = jnp.exp(pair * (-2.0 * math.log(rope_base) / HEAD_DIMENSION))
    positions = place * tokens + lax.broadcasted_iota(jnp.int32, (tokens, 1), 0)
    angles = positions.astype(jnp.float32) * freqs
    r.cosine[...] = jnp.cos(angles)
    sine = jnp.sin(angles)
    r.sine[...] = jnp.where(lane < HEAD_DIMENSION // 2, -sine, sine)
    docs_row = jnp.concatenate([r.docs[0:1], r.docs[1:2]], axis=1)
    every = r.docs_all[...]
    starts = jnp.zeros(docs_row.shape, jnp.float32)
    for name in range(1, DOCS):
        count = jnp.sum(jnp.where(every < float(name), 1.0, 0.0), axis=0)
        count = jnp.sum(jnp.sum(count, axis=0, keepdims=True), axis=1, keepdims=True)
        starts = starts + jnp.where(docs_row == float(name), count, 0.0)
    group = r.starts.shape[1] // tokens
    for head in range(group):
        r.starts[:, head * tokens : (head + 1) * tokens] = starts

    full_copy(left, 0, 0, right).wait_recv()
    full_copy(left, 0, 4, right).start()
    full_copy(right, 1, 3, left).wait_recv()
    full_copy(right, 1, 5, left).start()

    row_copy(down, 0, N_Z, 0, up).wait_recv()
    row_copy(down, 0, quarter, 2, up).start()
    core_copy(down, 1).start()
    row_copy(up, 0, N_Z, 1, down).wait_recv()
    row_copy(up, quarter, quarter, 3, down).start()
    core_copy(up, 2).start()

    full_copy(left, 1, 1, right).wait_recv()
    full_copy(right, 0, 2, left).wait_recv()

    row_copy(far, 0, quarter, 2, up).wait_recv()
    row_copy(far, quarter, quarter, 3, down).wait_recv()
    core_copy(far, 3).start()

    full_copy(opposite, 0, 4, right).wait_recv()
    full_copy(opposite, 1, 5, left).wait_recv()
    core_copy(row, 0, other).wait_recv()
    core_copy(down, 1, other).wait_recv()
    core_copy(up, 2, other).wait_recv()
    core_copy(far, 3, other).wait_recv()

    rows_each = r.gathered.shape[0] // N_T
    out_width = r.gathered.shape[3]
    depth = rows_each * r.gathered.shape[1] * r.gathered.shape[2]
    for part in range(2):
        squares = jnp.zeros((half, 1), jnp.float32)
        for owner in range(N_T):
            stream = r.full[owner, part].astype(jnp.float32)
            squares = squares + jnp.sum(stream * stream, axis=1, keepdims=True)
        scale = lax.rsqrt(squares / (N_T * width) + epsilon)
        total = jnp.zeros((half, out_width), jnp.float32)
        for owner in range(N_T):
            stream = r.full[owner, part].astype(jnp.float32)
            gain = jnp.concatenate(
                [
                    r.attn_gain[tile : tile + 1]
                    for tile in range(owner * width // NS, (owner + 1) * width // NS)
                ],
                axis=1,
            )
            block = (stream * scale * gain).astype(jnp.bfloat16)
            piece = r.gathered[owner * rows_each : (owner + 1) * rows_each].reshape(
                depth, out_width
            )
            total = total + jnp.dot(block, piece, preferred_element_type=jnp.float32)
        rows = slice(part * half, (part + 1) * half)
        count = out_width // HEAD_DIMENSION
        for head in range(count):
            lanes = slice(head * HEAD_DIMENSION, (head + 1) * HEAD_DIMENSION)
            value = total[:, lanes]
            if head < count - 1:
                value = (
                    value * r.cosine[rows] + pltpu.roll(value, HEAD_DIMENSION // 2, 1) * r.sine[rows]
                )
            if head < count - 2:
                begin = head * tokens + part * half
                r.queries[:, begin : begin + half] = value.T.astype(jnp.bfloat16)
            elif head < count - 1:
                r.window[0, part] = value.astype(jnp.bfloat16)
            else:
                r.window[0, 2 + part] = value.T.astype(jnp.bfloat16)

    def finish():
        for copy in rs:
            copy.wait_send()
        full_copy(me, 0, 0, right).wait_send()
        full_copy(me, 1, 3, left).wait_send()
        full_copy(me, 1, 1, right).wait_send()
        full_copy(me, 0, 2, left).wait_send()
        full_copy(left, 0, 4, right).wait_send()
        full_copy(right, 1, 5, left).wait_send()
        row_copy(row, 0, N_Z, 0, up).wait_send()
        row_copy(row, 0, N_Z, 1, down).wait_send()
        row_copy(down, 0, quarter, 2, up).wait_send()
        row_copy(up, quarter, quarter, 3, down).wait_send()
        for number, owner in enumerate((row, down, up, far)):
            core_copy(owner, number).wait_send()
        hidden_out.wait()

    return finish


def attend_phase(r, me):
    number = r.queries.shape[1]
    tokens = 2 * r.window.shape[2]
    group = number // tokens
    scale = HEAD_DIMENSION ** (-0.5) / math.log(2.0)
    window = r.window
    def masked_scores(slot):
        keys = window[slot, :2].reshape(tokens, HEAD_DIMENSION)
        scores = scale * jnp.dot(keys, r.queries[...], preferred_element_type=jnp.float32)
        key_index = lax.broadcasted_iota(jnp.int32, (tokens, number), 0).astype(jnp.float32)
        usable = key_index >= (r.starts[...] - (tokens * (me - slot)).astype(jnp.float32))
        return scores, usable, key_index

    def weighted(slot, probs):
        values = jnp.concatenate(
            [
                window[slot, 2],
                window[slot, 3],
            ],
            axis=1,
        )
        return jnp.dot(values, probs.astype(jnp.bfloat16), preferred_element_type=jnp.float32)

    def attend_first():
        scores, usable, key_index = masked_scores(0)
        query_index = lax.rem(lax.broadcasted_iota(jnp.int32, (1, number), 1), tokens)
        query_index = query_index.astype(jnp.float32)
        scores = jnp.where(usable & (key_index <= query_index), scores, -1e30)
        top = jnp.max(scores, axis=0, keepdims=True)
        probs = jnp.exp2(scores - top)
        r.best[...] = top
        r.denom[...] = jnp.sum(probs, axis=0, keepdims=True)
        r.accum[...] = weighted(0, probs)

    def attend(slot):
        scores, usable, _ = masked_scores(slot)
        scores = jnp.where(usable, scores, -1e30)
        before = r.best[...]
        fresh = jnp.maximum(before, jnp.max(scores, axis=0, keepdims=True))
        fade = jnp.exp2(before - fresh)
        probs = jnp.exp2(scores - fresh)
        r.best[...] = fresh
        r.denom[...] = r.denom[...] * fade + jnp.sum(probs, axis=0, keepdims=True)
        r.accum[...] = r.accum[...] * fade + weighted(slot, probs)

    row = lax.div(me, N_Z)
    col = lax.rem(me, N_Z)
    inner = col < N_Z - 1
    forward = row * N_Z + lax.rem(col + 1, N_Z)
    backward = lax.rem(me + N_CTX - 1, N_CTX)
    across = lax.rem(me + N_Z, N_CTX)
    up_base = jnp.where(inner, 0, N_Z)
    up_shift = jnp.where(inner, 1, 1 - N_Z)

    def send_up(slot, part):
        return remote(
            window.at[slot, part],
            window.at[slot + up_shift, part],
            r.win_up_send.at[slot, part],
            r.win_recv_sem.at[slot + up_shift, part],
            context_peer(forward),
        )

    def send_down(slot, part):
        return remote(
            window.at[slot, part],
            window.at[slot - 1, part],
            r.win_down_send.at[slot, part],
            r.win_recv_sem.at[slot - 1, part],
            context_peer(backward),
        )

    def send_across(slot, part):
        return remote(
            window.at[slot, part],
            window.at[slot + N_Z, part],
            r.win_across_send.at[slot, part],
            r.win_recv_sem.at[slot + N_Z, part],
            context_peer(across),
        )

    for part in range(4):
        send_across(0, part).start()

        @pl.when(inner)
        def _():
            send_up(0, part).start()

    attend_first()

    visits = (8, 1, 7, 16, 9, 2, 6, 15, 10, 3, 14, 5, 17, 11, 13, 4, 12)
    goes_down = (6, 7, 8, 13, 14, 15, 16)
    goes_across = (1, 2, 3, 8, 9)

    def visit(step, carry):
        slot = jnp.int32(visits[0])
        for number_here, value in enumerate(visits):
            slot = jnp.where(step == number_here, value, slot)
        upward = (slot >= up_base) & (slot <= up_base + 3)
        downward = ((slot >= 6) & (slot <= 8)) | ((slot >= 13) & (slot <= 16))
        crossing = (slot <= 3) | (slot == 8) | (slot == 9)
        for part in range(4):
            remote(
                window.at[slot, part],
                window.at[slot, part],
                r.win_down_send.at[slot, part],
                r.win_recv_sem.at[slot, part],
                context_peer(forward),
            ).wait_recv()

            @pl.when(crossing)
            def _():
                send_across(slot, part).start()

            @pl.when(upward)
            def _():
                send_up(slot, part).start()

            @pl.when(downward)
            def _():
                send_down(slot, part).start()

        attend(slot)
        return carry

    lax.fori_loop(0, len(visits), visit, 0)

    owner_row = lax.dot_general(
        r.owners[...].astype(jnp.float32),
        jnp.where(
            lax.div(lax.broadcasted_iota(jnp.int32, (N_CTX, tokens), 1), tokens // N_CTX)
            == lax.broadcasted_iota(jnp.int32, (N_CTX, tokens), 0),
            1.0,
            0.0,
        ),
        (((1,), (0,)), ((), ())),
        preferred_element_type=jnp.float32,
    )
    inside = lax.rem(lax.broadcasted_iota(jnp.int32, (1, tokens), 1), tokens // N_CTX)
    target_row = owner_row * (tokens // N_CTX) + inside.astype(jnp.float32)
    order = lax.broadcasted_iota(jnp.int32, (tokens, tokens), 0).astype(jnp.float32)
    chosen = jnp.where(order == target_row, 1.0, 0.0).astype(jnp.bfloat16)
    result = r.accum[...] / r.denom[...]
    for head in range(group):
        lanes = slice(head * HEAD_DIMENSION, (head + 1) * HEAD_DIMENSION)
        context = result[:, head * tokens : (head + 1) * tokens].astype(jnp.bfloat16)
        r.outgoing[:, :, lanes] = (
            lax.dot_general(
                chosen, context, (((1,), (1,)), ((), ())), preferred_element_type=jnp.float32
            )
            .reshape(N_CTX, tokens // N_CTX, HEAD_DIMENSION)
            .astype(jnp.bfloat16)
        )

    def row_copy(target, slot, step):
        return remote(
            r.outgoing.at[target],
            r.out_ref.at[slot],
            r.out_send.at[step],
            r.out_recv.at[slot],
            context_peer(target),
        )

    around(1, N_CTX, lambda step: row_copy(lax.rem(me + step, N_CTX), me, step).start())
    own_rows = pltpu.make_async_copy(r.outgoing.at[me], r.out_ref.at[me], r.out_sem.at[1])
    own_rows.start()
    for part in range(4):
        for slot in range(4):
            send_up(slot + up_base, part).wait_send()
        for slot in goes_down:
            send_down(slot, part).wait_send()
        for slot in (0,) + goes_across:
            send_across(slot, part).wait_send()

    def finish():
        def one(step):
            source = lax.rem(me + step, N_CTX)
            row_copy(source, source, step).wait_recv()
            row_copy(source, source, step).wait_send()

        around(1, N_CTX, one)
        own_rows.wait()

    return finish


def layer(
    mixer,
    gate,
    dt,
    docs,
    taps,
    conv_bias,
    small,
    gain,
    attn_gain,
    w_out,
    residual,
    w_query,
    w_key,
    w_value,
    owners,
):
    rows, channels = mixer.shape
    heads = dt.shape[0]
    width = heads * P_SIZE
    share = residual.shape[1]
    half = rows // 2
    widths = (w_query.shape[1], w_key.shape[1], w_value.shape[1])
    total_width = sum(widths)
    shard_rows = w_query.shape[0] // 2
    group = widths[0] // HEAD_DIMENSION
    out_rows = (N_CTX, rows // N_CTX, widths[0])
    bf, f32 = jnp.bfloat16, jnp.float32
    state = (N_CTX, width // N_CTX, NS)
    piece = VMEM((half, share), bf)
    scratch = dict(
        mixer=VMEM(mixer.shape, bf),
        gate=VMEM(gate.shape, bf),
        dt=VMEM(dt.shape, f32),
        docs=VMEM(docs.shape, f32),
        docs_raw=VMEM(docs.shape, jnp.int32),
        taps=VMEM(taps.shape, f32),
        conv_bias=VMEM(conv_bias.shape, f32),
        dt_bias=VMEM((1, heads), f32),
        a_log=VMEM((1, heads), f32),
        d_skip=VMEM((1, heads), f32),
        gain=VMEM(gain.shape, f32),
        attn_gain=VMEM(attn_gain.shape, f32),
        residual=VMEM(residual.shape, bf),
        owners=VMEM(owners.shape, jnp.int32),
        shard=VMEM((shard_rows, total_width), bf),
        w_tiles=VMEM((N_T, w_out.shape[0], share), bf),
        load_sem=DMA((16,)),
        tile_sem=DMA((N_T,)),
        out_sem=DMA((2,)),
        extended=VMEM((rows + 8, channels), f32),
        docs_ext=VMEM((rows + 8, NS), f32),
        halo=VMEM((16, channels), bf),
        halo_send=DMA((2,)),
        halo_recv=DMA((2,)),
        conv=VMEM((rows, channels), bf),
        side=VMEM((N_CTX, 1, NS), f32),
        side_all=VMEM((N_CTX, 1, NS), f32),
        docs_all=VMEM((N_CTX,) + docs.shape, f32),
        docs_send=DMA((N_CTX,)),
        docs_recv=DMA((N_CTX,)),
        pieces=VMEM(state, bf),
        recv=VMEM(state, bf),
        scanned=VMEM(state, bf),
        incoming=VMEM(state, bf),
        base=VMEM((rows, width), f32),
        swish=VMEM((rows, width), f32),
        normed=VMEM((rows, width), bf),
        shards=VMEM((N_Z, shard_rows, total_width), bf),
        send1=DMA((N_CTX,)),
        recv1=DMA((N_CTX,)),
        send2=DMA((N_CTX,)),
        recv2=DMA((N_CTX,)),
        send3=DMA((N_CTX,)),
        recv3=DMA((N_CTX,)),
        up_send=DMA((4,)),
        up_recv=DMA((4,)),
        down_send=DMA((4,)),
        down_recv=DMA((4,)),
        relay_a=piece,
        relay_b=piece,
        accum_a=piece,
        accum_b=piece,
        direct_a=piece,
        direct_b=piece,
        stage=VMEM((6, half, share), bf),
        hold_a=VMEM((half, share), f32),
        hold_b=VMEM((half, share), f32),
        full=VMEM((N_T, 2, half, share), bf),
        gathered=VMEM((N_CTX, 2, shard_rows, total_width), bf),
        cosine=VMEM((rows, HEAD_DIMENSION), f32),
        sine=VMEM((rows, HEAD_DIMENSION), f32),
        starts=VMEM((1, group * rows), f32),
        rs_send=DMA((6,)),
        rs_recv=DMA((6,)),
        ag_send=DMA((6,)),
        ag_recv=DMA((6,)),
        y_send=DMA((4,)),
        y_recv=DMA((4,)),
        core_send=DMA((4,)),
        core_recv=DMA((4,)),
        queries=VMEM((HEAD_DIMENSION, group * rows), bf),
        window=VMEM((WINDOW, 4, half, HEAD_DIMENSION), bf),
        outgoing=VMEM(out_rows, bf),
        best=VMEM((1, group * rows), f32),
        denom=VMEM((1, group * rows), f32),
        accum=VMEM((HEAD_DIMENSION, group * rows), f32),
        win_up_send=DMA((WINDOW, 4)),
        win_down_send=DMA((WINDOW, 4)),
        win_across_send=DMA((WINDOW, 4)),
        win_recv_sem=DMA((WINDOW, 4)),
        out_send=DMA((N_CTX,)),
        out_recv=DMA((N_CTX,)),
    )
    names = [
        "mixer_in",
        "gate_in",
        "dt_in",
        "docs_in",
        "taps_in",
        "conv_bias_in",
        "dt_bias_in",
        "a_log_in",
        "d_skip_in",
        "gain_in",
        "attn_gain_in",
        "w_out",
        "residual_in",
        "w_query",
        "w_key",
        "w_value",
        "owners_in",
        "hidden_ref",
        "out_ref",
    ] + list(scratch)

    def kernel(*refs):
        r = SimpleNamespace(**dict(zip(names, refs)))
        me = lax.axis_index("context")
        here = lax.axis_index("tensor")
        core = lax.axis_index("dp")
        barrier = pltpu.get_barrier_semaphore()

        def signal(peer):
            pl.semaphore_signal(barrier, inc=1, device_id=peer, device_id_type=MESH)

        around(1, N_CTX, lambda step: signal(context_peer(lax.rem(me + step, N_CTX))))
        signal(tensor_peer(lax.rem(here + 1, N_T)))
        signal(tensor_peer(lax.rem(here + 3, N_T)))
        signal({"dp": 1 - core})

        def load(src, dst, number):
            copy = pltpu.make_async_copy(src, dst, r.load_sem.at[number])
            copy.start()
            return copy

        r.load_docs = load(r.docs_in, r.docs_raw, 0)
        r.load_taps = load(r.taps_in, r.taps, 1)
        r.load_conv_bias = load(r.conv_bias_in, r.conv_bias, 10)
        r.load_small = [
            load(r.dt_bias_in, r.dt_bias, 11),
            load(r.a_log_in, r.a_log, 12),
            load(r.d_skip_in, r.d_skip, 13),
        ]
        r.load_mixer = load(r.mixer_in, r.mixer, 2)
        r.load_dt = load(r.dt_in, r.dt, 3)
        half_rows = pl.ds(core * shard_rows, shard_rows)
        r.load_shard = []
        begin = 0
        for number, (source, count) in enumerate(zip((r.w_query, r.w_key, r.w_value), widths)):
            r.load_shard.append(
                load(source.at[half_rows], r.shard.at[:, pl.ds(begin, count)], 4 + number)
            )
            begin += count
        r.load_gate = load(r.gate_in, r.gate, 7)
        r.load_gain = load(r.gain_in, r.gain, 14)
        r.load_attn_gain = load(r.attn_gain_in, r.attn_gain, 15)
        r.load_residual = load(r.residual_in, r.residual, 8)
        load_owners = load(r.owners_in, r.owners, 9)
        r.load_tiles = []
        for number, owner in enumerate((here + 2, here + 1, here + 3, here)):
            column = pl.multiple_of(lax.rem(owner, N_T) * share, share)
            copy = pltpu.make_async_copy(
                r.w_out.at[:, pl.ds(column, share)], r.w_tiles.at[number], r.tile_sem.at[number]
            )
            copy.start()
            r.load_tiles.append(copy)

        finish_mix, shards_arrive = mix_phase(r, me, core)
        finish_project = project_phase(r, me, core, shards_arrive)
        load_owners.wait()
        finish_attend = attend_phase(r, me)
        finish_mix()
        finish_project()
        finish_attend()

    anywhere = pl.BlockSpec(memory_space=pl.ANY)
    return pl.pallas_call(
        kernel,
        out_shape=(
            jax.ShapeDtypeStruct((2, half, share), bf),
            jax.ShapeDtypeStruct(out_rows, bf),
        ),
        in_specs=[anywhere] * 17,
        out_specs=(anywhere, anywhere),
        scratch_shapes=list(scratch.values()),
        compiler_params=pltpu.CompilerParams(
            collective_id=0, has_side_effects=True, vmem_limit_bytes=60 * 1024 * 1024
        ),
        name="layer",
    )(
        mixer,
        gate,
        dt,
        docs,
        taps,
        conv_bias,
        *small,
        gain,
        attn_gain,
        w_out,
        residual,
        w_query,
        w_key,
        w_value,
        owners,
    )


def per_device(
    mixer_input,
    gate_z,
    dt_raw,
    dt_bias,
    a_log,
    d_skip,
    conv_weight,
    conv_bias,
    norm_gain,
    w_out,
    residual,
    attn_gain,
    w_query,
    w_key,
    value_weight,
    doc_ids,
    owners,
):
    row_count, channels = mixer_input.shape
    share = residual.shape[1]

    hidden_out, attended = layer(
        mixer_input,
        gate_z,
        dt_raw.T,
        doc_ids.reshape(row_count // NS, NS),
        conv_weight,
        conv_bias.reshape(channels // NS, NS),
        (dt_bias[None, :], a_log[None, :], d_skip[None, :]),
        norm_gain[None, :],
        attn_gain.reshape(-1, NS),
        w_out,
        residual,
        w_query,
        w_key,
        value_weight,
        owners,
    )
    return (
        hidden_out.reshape(row_count, share),
        attended.reshape(row_count, w_query.shape[1]),
    )


def solution(mesh):
    in_specs = (
        P(("dp", "context"), "tensor"),
        P(("dp", "context"), "tensor"),
        P(("dp", "context"), "tensor"),
        P("tensor"),
        P("tensor"),
        P("tensor"),
        P(None, "tensor"),
        P("tensor"),
        P("tensor"),
        P("tensor", None),
        P(("dp", "context"), "tensor"),
        P(),
        P("context", "tensor"),
        P("context", "tensor"),
        P("context", "tensor"),
        P(("dp", "context")),
        P(("dp", "context"), None),
    )
    out_specs = (P(("dp", "context"), "tensor"), P(("dp", "context"), "tensor"))
    return jax.shard_map(
        per_device, mesh=mesh, in_specs=in_specs, out_specs=out_specs, check_vma=False
    )
```

```python
import math
from types import SimpleNamespace

import jax
import jax.numpy as jnp
from jax import lax
from jax.experimental import pallas as pl
from jax.experimental.pallas import tpu as pltpu
from jax.sharding import PartitionSpec as P

P_SIZE = 64
NS = 128
HEAD_DIMENSION = 128
N_CTX = 32
N_Y = 4
N_Z = 8
N_T = 4
WINDOW = 18
DOCS = 16

epsilon = 1e-05
rope_base = 500000.0
MESH = pl.DeviceIdType.MESH
VMEM = pltpu.VMEM
DMA = pltpu.SemaphoreType.DMA


def context_peer(index):
    return {"context": index}


def tensor_peer(index):
    return {"tensor": index}


def remote(src, dst, send_sem, recv_sem, peer):
    return pltpu.make_async_remote_copy(
        src_ref=src,
        dst_ref=dst,
        send_sem=send_sem,
        recv_sem=recv_sem,
        device_id=peer,
        device_id_type=MESH,
    )


def softplus(value):
    return jnp.maximum(value, 0.0) + jnp.log1p(jnp.exp(-jnp.abs(value)))


def around(first, count, step, carry=None):
    lax.fori_loop(first, count, lambda number, none: (step(number), none)[1], 0)


def cross_copy(r, row, col, core, place, direction, source=None):
    target = lax.rem(row + (1 if direction == 0 else N_Y - 1), N_Y)
    return remote(
        r.shards.at[place] if source is None else source,
        r.gathered.at[row * N_Z + place, core],
        r.cross_send.at[direction, place],
        r.cross_recv.at[direction, place],
        context_peer(target * N_Z + col),
    )


def mix_phase(r, me, core):
    row = lax.div(me, N_Z)
    col = lax.rem(me, N_Z)
    above = context_peer(row * N_Z + lax.rem(col + 1, N_Z))
    below = context_peer(row * N_Z + lax.rem(col + N_Z - 1, N_Z))
    rows, channels = r.mixer.shape
    heads = r.dt.shape[0]
    width = heads * P_SIZE
    pairs = width // NS
    exact = lax.Precision.HIGHEST
    pad = 8
    edge = 16

    r.load_docs.wait()
    r.docs[...] = r.docs_raw[...].astype(jnp.float32)
    docs_row = jnp.concatenate([r.docs[0:1], r.docs[1:2]], axis=1)
    first = lax.broadcasted_iota(jnp.int32, (rows, rows), 0)
    second = lax.broadcasted_iota(jnp.int32, (rows, rows), 1)
    unit = jnp.where(first == second, 1.0, 0.0)
    nt = (((1,), (1,)), ((), ()))

    def turned(value, precision):
        return lax.dot_general(
            unit, value, nt, precision=precision, preferred_element_type=jnp.float32
        )

    docs_col = turned(jnp.broadcast_to(docs_row, (NS, rows)), exact)
    r.docs_ext[pad:] = docs_col

    r.load_taps.wait()
    r.load_conv_bias.wait()
    r.load_mixer.wait()
    r.extended[pad:] = r.mixer[...].astype(jnp.float32)

    def convolve(begin, count):
        here = r.docs_ext[pad + begin : pad + begin + count]
        masks = [
            jnp.where(
                r.docs_ext[pad - 3 + k + begin : pad - 3 + k + begin + count] == here, 1.0, 0.0
            )
            for k in range(3)
        ]
        for chunk in range(channels // NS):
            lanes = slice(chunk * NS, (chunk + 1) * NS)
            running = r.conv_bias[chunk : chunk + 1] + r.taps[3:4, lanes] * (
                r.extended[pad + begin : pad + begin + count, lanes]
            )
            for k in range(3):
                start = pad - 3 + k + begin
                running = running + r.taps[k : k + 1, lanes] * (
                    masks[k] * r.extended[start : start + count, lanes]
                )
            r.conv[begin : begin + count, lanes] = (running * jax.nn.sigmoid(running)).astype(
                jnp.bfloat16
            )

    convolve(edge, rows - edge)

    r.load_dt.wait()
    for small in r.load_small:
        small.wait()
    diagonal = lax.broadcasted_iota(jnp.int32, (heads, heads), 0) == lax.broadcasted_iota(
        jnp.int32, (heads, heads), 1
    )

    def column(ref):
        return jnp.sum(jnp.where(diagonal, ref[...], 0.0), axis=1, keepdims=True)

    bias, rate, skip = column(r.dt_bias), column(r.a_log), column(r.d_skip)
    step_turned = softplus(r.dt[...] + bias)
    cumul_turned = jnp.dot(
        -step_turned * jnp.exp(rate),
        jnp.where(first <= second, 1.0, 0.0),
        precision=exact,
        preferred_element_type=jnp.float32,
    )
    last_doc = docs_row[:, rows - 1 : rows]
    end_turned = (
        jnp.exp(cumul_turned[:, rows - 1 : rows] - cumul_turned)
        * jnp.where(docs_row == last_doc, 1.0, 0.0)
        * step_turned
    )
    cumul = turned(cumul_turned, exact)
    end_weight = turned(end_turned, exact)
    begin_weight = jnp.exp(cumul)
    lower = lax.broadcasted_iota(jnp.int32, (rows, NS), 1) < P_SIZE

    def spread(value, pair):
        return jnp.where(
            lower, value[:, 2 * pair : 2 * pair + 1], value[:, 2 * pair + 1 : 2 * pair + 2]
        )

    pl.semaphore_wait(pltpu.get_barrier_semaphore(), N_CTX - 1 + 3)

    following = context_peer(lax.rem(me + 1, N_CTX))
    halo_rows = remote(
        r.mixer.at[pl.ds(rows - edge, edge)], r.halo, r.halo_send.at[0], r.halo_recv.at[0], following
    )
    halo_docs = remote(
        r.docs_ext.at[pl.ds(rows, pad)],
        r.docs_ext.at[pl.ds(0, pad)],
        r.halo_send.at[1],
        r.halo_recv.at[1],
        following,
    )
    halo_docs.start()
    halo_rows.start()

    def docs_copy(target, slot, number):
        return remote(
            r.docs,
            r.docs_all.at[slot],
            r.docs_send.at[number],
            r.docs_recv.at[slot],
            context_peer(target),
        )

    for load in r.load_shard:
        load.wait()

    def shard_copy(place, distance, sends, recvs, target):
        return remote(
            r.shard if distance == 0 else r.shards.at[place],
            r.shards.at[place],
            sends.at[distance],
            recvs.at[distance],
            target,
        )

    def shard_up(distance):
        place = lax.rem(col + N_Z - distance, N_Z)
        return shard_copy(place, distance, r.up_send, r.up_recv, above)

    def shard_down(distance):
        place = lax.rem(col + distance, N_Z)
        return shard_copy(place, distance, r.down_send, r.down_recv, below)

    def spread_shard(place):
        cross_copy(r, row, col, core, place, 0).start()
        cross_copy(r, row, col, core, place, 1).start()

    halo_docs.wait_recv()
    r.docs_ext[:pad] = jnp.where(me > 0, r.docs_ext[:pad], -1.0)
    halo_rows.wait_recv()
    r.extended[:pad] = r.halo[edge - pad :].astype(jnp.float32)
    convolve(0, edge)
    in_b = r.conv[:, width : width + NS]
    out_c = r.conv[:, width + NS :]
    prev_doc = r.docs_ext[pad - 1 : pad]
    carry_on = jnp.where(r.docs_ext[pad:] == prev_doc, 1.0, 0.0)
    through = jnp.exp(cumul_turned[:, rows - 1 : rows]) * jnp.where(
        last_doc == prev_doc[:, 0:1], 1.0, 0.0
    )

    each = N_CTX // pairs
    for pair in range(pairs):
        lanes = slice(pair * NS, (pair + 1) * NS)
        scaled = (r.conv[:, lanes].astype(jnp.float32) * spread(end_weight, pair)).astype(
            jnp.bfloat16
        )
        state = lax.dot_general(
            scaled, in_b, (((0,), (0,)), ((), ())), preferred_element_type=jnp.float32
        )
        r.pieces[pair * each : (pair + 1) * each] = state.reshape(
            each, NS // each, NS
        ).astype(jnp.bfloat16)
    for head in range(heads):
        for part in range(N_CTX // heads):
            r.side[head * (N_CTX // heads) + part] = jnp.broadcast_to(
                through[head : head + 1], (1, NS)
            )

    def piece_copy(target, slot, number):
        return remote(
            r.pieces.at[target],
            r.recv.at[slot],
            r.send1.at[number],
            r.recv1.at[slot],
            context_peer(target),
        )

    def side_copy(target, slot, number):
        return remote(
            r.side.at[target],
            r.side_all.at[slot],
            r.send2.at[number],
            r.recv2.at[slot],
            context_peer(target),
        )

    def back_copy(target, slot, number):
        return remote(
            r.scanned.at[target],
            r.incoming.at[slot],
            r.send3.at[number],
            r.recv3.at[slot],
            context_peer(target),
        )

    def start_out(number):
        target = lax.rem(me + number, N_CTX)
        side_copy(target, me, number).start()
        piece_copy(target, me, number).start()

    around(1, N_CTX, start_out)
    shard_up(0).start()
    shard_down(0).start()
    around(1, N_CTX, lambda number: docs_copy(lax.rem(me + number, N_CTX), me, number).start())
    r.docs_all[me] = r.docs[...]
    r.recv[me] = r.pieces[me]
    r.side_all[me] = r.side[me]
    r.shards[col] = r.shard[...]
    cross_copy(r, row, col, core, col, 0, r.shard).start()
    cross_copy(r, row, col, core, col, 1, r.shard).start()

    mixing = lax.dot_general(out_c, in_b, nt, preferred_element_type=jnp.float32)
    docs_wide = jnp.concatenate([docs_col, docs_col], axis=1)
    mixing = jnp.where((first >= second) & (docs_wide == docs_row), mixing, 0.0)
    for pair in range(pairs):
        lanes = slice(pair * NS, (pair + 1) * NS)
        inputs = r.conv[:, lanes]
        results = []
        for head in (2 * pair, 2 * pair + 1):
            fall = jnp.minimum(
                cumul[:, head : head + 1] - cumul_turned[head : head + 1], 0.0
            )
            weight = jnp.exp(fall) * mixing * step_turned[head : head + 1]
            results.append(
                jnp.dot(
                    weight.astype(jnp.bfloat16), inputs, preferred_element_type=jnp.float32
                )
            )
        r.base[:, lanes] = jnp.where(lower, results[0], results[1]) + jnp.where(
            lower[0:1], skip[2 * pair : 2 * pair + 1], skip[2 * pair + 1 : 2 * pair + 2]
        ) * inputs.astype(jnp.float32)

    def arrive(number):
        source = lax.rem(me + number, N_CTX)
        side_copy(source, source, number).wait_recv()
        piece_copy(source, source, number).wait_recv()

    around(1, N_CTX, arrive)

    def one(turn, state):
        r.scanned[turn] = state.astype(jnp.bfloat16)
        return state * r.side_all[turn] + r.recv[turn].astype(
            jnp.float32
        )

    lax.fori_loop(0, N_CTX, one, jnp.zeros(r.recv.shape[1:], jnp.float32))
    r.incoming[me] = r.scanned[me]

    def start_back(number):
        back_copy(lax.rem(me + number, N_CTX), me, number).start()

    around(1, N_CTX, start_back)

    def shard_turn(distance):
        shard_up(distance - 1).wait_recv()
        shard_up(distance).start()
        if distance < 3:
            shard_down(distance - 1).wait_recv()
            shard_down(distance).start()
            spread_shard(lax.rem(col + distance, N_Z))
        spread_shard(lax.rem(col + N_Z - distance, N_Z))

    shard_turn(1)
    r.load_gate.wait()
    gated_by = r.gate[...].astype(jnp.float32)
    r.swish[...] = gated_by * jax.nn.sigmoid(gated_by)
    shard_turn(2)

    def returned(number):
        source = lax.rem(me + number, N_CTX)
        back_copy(source, source, number).wait_recv()

    around(1, N_CTX, returned)
    shard_turn(3)
    squares = jnp.zeros((rows, 1), jnp.float32)
    for pair in range(pairs):
        lanes = slice(pair * NS, (pair + 1) * NS)
        carried = r.incoming[pair * each : (pair + 1) * each].reshape(NS, NS)
        arrived = lax.dot_general(out_c, carried, nt, preferred_element_type=jnp.float32)
        gated = (
            r.base[:, lanes] + spread(begin_weight, pair) * carry_on * arrived
        ) * r.swish[:, lanes]
        r.base[:, lanes] = gated
        squares = squares + jnp.sum(gated * gated, axis=1, keepdims=True)
    scale = lax.rsqrt(squares / width + epsilon)
    r.load_gain.wait()
    r.normed[...] = (r.base[...] * scale * r.gain[...]).astype(jnp.bfloat16)

    def finish():
        def sent(number):
            source = lax.rem(me + number, N_CTX)
            piece_copy(source, source, number).wait_send()
            side_copy(source, source, number).wait_send()
            docs_copy(source, source, number).wait_send()
            back_copy(source, source, number).wait_send()

        around(1, N_CTX, sent)
        halo_rows.wait_send()
        halo_docs.wait_send()
        for distance in range(4):
            shard_up(distance).wait_send()
            if distance < 3:
                shard_down(distance).wait_send()

    def docs_arrive(number):
        source = lax.rem(me + number, N_CTX)
        docs_copy(source, source, number).wait_recv()

    def shards_arrive():
        shard_down(2).wait_recv()
        spread_shard(lax.rem(col + 3, N_Z))
        shard_up(3).wait_recv()
        spread_shard(lax.rem(col + 4, N_Z))
        around(1, N_CTX, docs_arrive)

    return finish, shards_arrive


def project_phase(r, me_context, core, shards_arrive):
    me = lax.axis_index("tensor")
    place = me_context
    other = 1 - core
    right = lax.rem(me + 1, N_T)
    left = lax.rem(me + 3, N_T)
    opposite = lax.rem(me + 2, N_T)
    row = lax.div(place, N_Z)
    col = lax.rem(place, N_Z)
    up = lax.rem(row + 1, N_Y)
    down = lax.rem(row + 3, N_Y)
    far = lax.rem(row + 2, N_Y)
    width = r.residual.shape[1]
    tokens = r.residual.shape[0]
    half = tokens // 2

    def multiply(number):
        r.load_tiles[number].wait()
        return jnp.dot(r.normed[...], r.w_tiles[number], preferred_element_type=jnp.float32)

    rs = [
        remote(r.stage.at[0], r.relay_a, r.rs_send.at[0], r.rs_recv.at[0], tensor_peer(right)),
        remote(r.stage.at[1], r.relay_b, r.rs_send.at[1], r.rs_recv.at[1], tensor_peer(left)),
        remote(r.stage.at[2], r.direct_b, r.rs_send.at[2], r.rs_recv.at[2], tensor_peer(right)),
        remote(r.stage.at[3], r.direct_a, r.rs_send.at[3], r.rs_recv.at[3], tensor_peer(left)),
        remote(r.stage.at[4], r.accum_a, r.rs_send.at[4], r.rs_recv.at[4], tensor_peer(right)),
        remote(r.stage.at[5], r.accum_b, r.rs_send.at[5], r.rs_recv.at[5], tensor_peer(left)),
    ]
    product = multiply(0)
    r.stage[0] = product[:half].astype(jnp.bfloat16)
    r.stage[1] = product[half:].astype(jnp.bfloat16)
    rs[0].start()
    rs[1].start()

    quarter = N_Z // 2

    def row_copy(owner_row, begin, count, number, target_row):
        part = r.gathered.at[pl.ds(owner_row * N_Z + begin, count), core]
        return remote(
            part,
            part,
            r.y_send.at[number],
            r.y_recv.at[number],
            context_peer(target_row * N_Z + col),
        )

    def core_copy(owner_row, number, side=core, source=None):
        part = r.gathered.at[pl.ds(owner_row * N_Z, N_Z), side]
        return remote(
            part if source is None else source,
            part,
            r.core_send.at[number],
            r.core_recv.at[number],
            {"dp": other},
        )

    product = multiply(1)
    r.stage[2] = product[half:].astype(jnp.bfloat16)
    r.hold_a[...] = product[:half]
    rs[2].start()
    product = multiply(2)
    r.stage[3] = product[:half].astype(jnp.bfloat16)
    r.hold_b[...] = product[half:]
    rs[3].start()

    shards_arrive()
    core_copy(row, 0, core, r.shards).start()

    rs[0].wait_recv()
    r.stage[4] = (r.hold_a[...] + r.relay_a[...].astype(jnp.float32)).astype(jnp.bfloat16)
    rs[4].start()
    rs[1].wait_recv()
    r.stage[5] = (r.hold_b[...] + r.relay_b[...].astype(jnp.float32)).astype(jnp.bfloat16)
    rs[5].start()
    product = multiply(3)
    r.hold_a[...] = product[:half]
    r.hold_b[...] = product[half:]
    r.gathered[pl.ds(row * N_Z, N_Z), core] = r.shards[...]
    around(0, N_Z, lambda place: cross_copy(r, down, col, core, place, 0).wait_recv())
    row_copy(down, 0, quarter, 2, up).start()
    core_copy(down, 1).start()
    around(0, N_Z, lambda place: cross_copy(r, up, col, core, place, 1).wait_recv())
    row_copy(up, quarter, quarter, 3, down).start()
    core_copy(up, 2).start()

    def full_copy(owner, part, number, target):
        return remote(
            r.full.at[owner, part],
            r.full.at[owner, part],
            r.ag_send.at[number],
            r.ag_recv.at[number],
            tensor_peer(target),
        )

    r.load_residual.wait()
    r.load_attn_gain.wait()
    rs[3].wait_recv()
    rs[4].wait_recv()
    r.full[me, 0] = (
        r.residual[:half].astype(jnp.float32)
        + (
            r.hold_a[...]
            + (r.direct_a[...].astype(jnp.float32) + r.accum_a[...].astype(jnp.float32))
        )
    ).astype(jnp.bfloat16)
    full_copy(me, 0, 0, right).start()
    full_copy(me, 0, 2, left).start()
    rs[2].wait_recv()
    rs[5].wait_recv()
    r.full[me, 1] = (
        r.residual[half:].astype(jnp.float32)
        + (
            r.hold_b[...]
            + (r.direct_b[...].astype(jnp.float32) + r.accum_b[...].astype(jnp.float32))
        )
    ).astype(jnp.bfloat16)
    full_copy(me, 1, 3, left).start()
    full_copy(me, 1, 1, right).start()
    hidden_out = pltpu.make_async_copy(r.full.at[me], r.hidden_ref, r.out_sem.at[0])
    hidden_out.start()

    lane = lax.broadcasted_iota(jnp.int32, (1, HEAD_DIMENSION), 1)
    pair = lax.rem(lane, HEAD_DIMENSION // 2).astype(jnp.float32)
    freqs = jnp.exp(pair * (-2.0 * math.log(rope_base) / HEAD_DIMENSION))
    positions = place * tokens + lax.broadcasted_iota(jnp.int32, (tokens, 1), 0)
    angles = positions.astype(jnp.float32) * freqs
    r.cosine[...] = jnp.cos(angles)
    sine = jnp.sin(angles)
    r.sine[...] = jnp.where(lane < HEAD_DIMENSION // 2, -sine, sine)
    docs_row = jnp.concatenate([r.docs[0:1], r.docs[1:2]], axis=1)
    every = r.docs_all[...]
    starts = jnp.zeros(docs_row.shape, jnp.float32)
    for name in range(1, DOCS):
        count = jnp.sum(jnp.where(every < float(name), 1.0, 0.0), axis=0)
        count = jnp.sum(jnp.sum(count, axis=0, keepdims=True), axis=1, keepdims=True)
        starts = starts + jnp.where(docs_row == float(name), count, 0.0)
    group = r.starts.shape[1] // tokens
    for head in range(group):
        r.starts[:, head * tokens : (head + 1) * tokens] = starts

    full_copy(left, 0, 0, right).wait_recv()
    full_copy(left, 0, 4, right).start()
    full_copy(right, 1, 3, left).wait_recv()
    full_copy(right, 1, 5, left).start()

    full_copy(left, 1, 1, right).wait_recv()
    full_copy(right, 0, 2, left).wait_recv()

    row_copy(far, 0, quarter, 2, up).wait_recv()
    row_copy(far, quarter, quarter, 3, down).wait_recv()
    core_copy(far, 3).start()

    full_copy(opposite, 0, 4, right).wait_recv()
    full_copy(opposite, 1, 5, left).wait_recv()
    core_copy(row, 0, other).wait_recv()
    core_copy(down, 1, other).wait_recv()
    core_copy(up, 2, other).wait_recv()
    core_copy(far, 3, other).wait_recv()

    rows_each = r.gathered.shape[0] // N_T
    out_width = r.gathered.shape[3]
    depth = rows_each * r.gathered.shape[1] * r.gathered.shape[2]
    for part in range(2):
        squares = jnp.zeros((half, 1), jnp.float32)
        for owner in range(N_T):
            stream = r.full[owner, part].astype(jnp.float32)
            squares = squares + jnp.sum(stream * stream, axis=1, keepdims=True)
        scale = lax.rsqrt(squares / (N_T * width) + epsilon)
        for owner in range(N_T):
            stream = r.full[owner, part].astype(jnp.float32)
            gain = jnp.concatenate(
                [
                    r.attn_gain[tile : tile + 1]
                    for tile in range(owner * width // NS, (owner + 1) * width // NS)
                ],
                axis=1,
            )
            r.block[part, owner] = (stream * scale * gain).astype(jnp.bfloat16)
    pair_begin = out_width - 2 * HEAD_DIMENSION

    def product_of(part, begin, count):
        total = jnp.zeros((half, count), jnp.float32)
        for owner in range(N_T):
            piece = r.gathered[
                owner * rows_each : (owner + 1) * rows_each, :, :, begin : begin + count
            ].reshape(depth, count)
            total = total + jnp.dot(
                r.block[part, owner], piece, preferred_element_type=jnp.float32
            )
        return total

    def turn(value, rows):
        return value * r.cosine[rows] + pltpu.roll(value, HEAD_DIMENSION // 2, 1) * r.sine[rows]

    for part in range(2):
        rows = slice(part * half, (part + 1) * half)
        total = product_of(part, pair_begin, 2 * HEAD_DIMENSION)
        r.window[0, part] = turn(total[:, :HEAD_DIMENSION], rows).astype(jnp.bfloat16)
        r.window[0, 2 + part] = total[:, HEAD_DIMENSION:].T.astype(jnp.bfloat16)

    def make_queries():
        for part in range(2):
            rows = slice(part * half, (part + 1) * half)
            total = product_of(part, 0, pair_begin)
            for head in range(pair_begin // HEAD_DIMENSION):
                value = turn(
                    total[:, head * HEAD_DIMENSION : (head + 1) * HEAD_DIMENSION], rows
                )
                begin = head * tokens + part * half
                r.queries[:, begin : begin + half] = value.T.astype(jnp.bfloat16)

    def finish():
        for copy in rs:
            copy.wait_send()
        full_copy(me, 0, 0, right).wait_send()
        full_copy(me, 1, 3, left).wait_send()
        full_copy(me, 1, 1, right).wait_send()
        full_copy(me, 0, 2, left).wait_send()
        full_copy(left, 0, 4, right).wait_send()
        full_copy(right, 1, 5, left).wait_send()

        def crossed(place):
            cross_copy(r, row, col, core, place, 0).wait_send()
            cross_copy(r, row, col, core, place, 1).wait_send()

        around(0, N_Z, crossed)
        row_copy(down, 0, quarter, 2, up).wait_send()
        row_copy(up, quarter, quarter, 3, down).wait_send()
        for number, owner in enumerate((row, down, up, far)):
            core_copy(owner, number).wait_send()
        hidden_out.wait()

    return finish, make_queries


def attend_phase(r, me, make_queries):
    number = r.queries.shape[1]
    tokens = 2 * r.window.shape[2]
    group = number // tokens
    scale = HEAD_DIMENSION ** (-0.5) / math.log(2.0)
    window = r.window
    def masked_scores(slot):
        keys = window[slot, :2].reshape(tokens, HEAD_DIMENSION)
        scores = scale * jnp.dot(keys, r.queries[...], preferred_element_type=jnp.float32)
        key_index = lax.broadcasted_iota(jnp.int32, (tokens, number), 0).astype(jnp.float32)
        usable = key_index >= (r.starts[...] - (tokens * (me - slot)).astype(jnp.float32))
        return scores, usable, key_index

    def weighted(slot, probs):
        values = jnp.concatenate(
            [
                window[slot, 2],
                window[slot, 3],
            ],
            axis=1,
        )
        return jnp.dot(values, probs.astype(jnp.bfloat16), preferred_element_type=jnp.float32)

    def attend_first():
        scores, usable, key_index = masked_scores(0)
        query_index = lax.rem(lax.broadcasted_iota(jnp.int32, (1, number), 1), tokens)
        query_index = query_index.astype(jnp.float32)
        scores = jnp.where(usable & (key_index <= query_index), scores, -1e30)
        top = jnp.max(scores, axis=0, keepdims=True)
        probs = jnp.exp2(scores - top)
        r.best[...] = top
        r.denom[...] = jnp.sum(probs, axis=0, keepdims=True)
        r.accum[...] = weighted(0, probs)

    def attend(slot):
        scores, usable, _ = masked_scores(slot)
        scores = jnp.where(usable, scores, -1e30)
        before = r.best[...]
        fresh = jnp.maximum(before, jnp.max(scores, axis=0, keepdims=True))
        fade = jnp.exp2(before - fresh)
        probs = jnp.exp2(scores - fresh)
        r.best[...] = fresh
        r.denom[...] = r.denom[...] * fade + jnp.sum(probs, axis=0, keepdims=True)
        r.accum[...] = r.accum[...] * fade + weighted(slot, probs)

    row = lax.div(me, N_Z)
    col = lax.rem(me, N_Z)
    inner = col < N_Z - 1
    forward = row * N_Z + lax.rem(col + 1, N_Z)
    backward = lax.rem(me + N_CTX - 1, N_CTX)
    across = lax.rem(me + N_Z, N_CTX)
    up_base = jnp.where(inner, 0, N_Z)
    up_shift = jnp.where(inner, 1, 1 - N_Z)

    def send_up(slot, part):
        return remote(
            window.at[slot, part],
            window.at[slot + up_shift, part],
            r.win_up_send.at[slot, part],
            r.win_recv_sem.at[slot + up_shift, part],
            context_peer(forward),
        )

    def send_down(slot, part):
        return remote(
            window.at[slot, part],
            window.at[slot - 1, part],
            r.win_down_send.at[slot, part],
            r.win_recv_sem.at[slot - 1, part],
            context_peer(backward),
        )

    def send_across(slot, part):
        return remote(
            window.at[slot, part],
            window.at[slot + N_Z, part],
            r.win_across_send.at[slot, part],
            r.win_recv_sem.at[slot + N_Z, part],
            context_peer(across),
        )

    for part in range(4):
        send_across(0, part).start()

        @pl.when(inner)
        def _():
            send_up(0, part).start()

    make_queries()
    attend_first()

    visits = (8, 1, 7, 16, 9, 2, 6, 15, 10, 3, 14, 5, 17, 11, 13, 4, 12)
    goes_down = (6, 7, 8, 13, 14, 15, 16)
    goes_across = (1, 2, 3, 8, 9)

    def visit(step, carry):
        slot = jnp.int32(visits[0])
        for number_here, value in enumerate(visits):
            slot = jnp.where(step == number_here, value, slot)
        upward = (slot >= up_base) & (slot <= up_base + 3)
        for part in range(4):
            remote(
                window.at[slot, part],
                window.at[slot, part],
                r.win_down_send.at[slot, part],
                r.win_recv_sem.at[slot, part],
                context_peer(forward),
            ).wait_recv()

            last_down, last_cross = (13, 3) if part < 2 else (14, 4)
            downward = ((slot >= 6) & (slot <= 8)) | ((slot >= last_down) & (slot <= 16))
            crossing = (slot <= last_cross) | (slot == 8) | (slot == 9)

            @pl.when(crossing)
            def _():
                send_across(slot, part).start()

            @pl.when(upward)
            def _():
                send_up(slot, part).start()

            @pl.when(downward)
            def _():
                send_down(slot, part).start()

        attend(slot)
        return carry

    lax.fori_loop(0, len(visits), visit, 0)

    owner_row = lax.dot_general(
        r.owners[...].astype(jnp.float32),
        jnp.where(
            lax.div(lax.broadcasted_iota(jnp.int32, (N_CTX, tokens), 1), tokens // N_CTX)
            == lax.broadcasted_iota(jnp.int32, (N_CTX, tokens), 0),
            1.0,
            0.0,
        ),
        (((1,), (0,)), ((), ())),
        preferred_element_type=jnp.float32,
    )
    inside = lax.rem(lax.broadcasted_iota(jnp.int32, (1, tokens), 1), tokens // N_CTX)
    target_row = owner_row * (tokens // N_CTX) + inside.astype(jnp.float32)
    order = lax.broadcasted_iota(jnp.int32, (tokens, tokens), 0).astype(jnp.float32)
    chosen = jnp.where(order == target_row, 1.0, 0.0).astype(jnp.bfloat16)
    result = r.accum[...] / r.denom[...]
    for head in range(group):
        lanes = slice(head * HEAD_DIMENSION, (head + 1) * HEAD_DIMENSION)
        context = result[:, head * tokens : (head + 1) * tokens].astype(jnp.bfloat16)
        r.outgoing[:, :, lanes] = (
            lax.dot_general(
                chosen, context, (((1,), (1,)), ((), ())), preferred_element_type=jnp.float32
            )
            .reshape(N_CTX, tokens // N_CTX, HEAD_DIMENSION)
            .astype(jnp.bfloat16)
        )

    def row_copy(target, slot, step):
        return remote(
            r.outgoing.at[target],
            r.out_ref.at[slot],
            r.out_send.at[step],
            r.out_recv.at[slot],
            context_peer(target),
        )

    around(1, N_CTX, lambda step: row_copy(lax.rem(me + step, N_CTX), me, step).start())
    own_rows = pltpu.make_async_copy(r.outgoing.at[me], r.out_ref.at[me], r.out_sem.at[1])
    own_rows.start()
    for part in range(4):
        for slot in range(4):
            send_up(slot + up_base, part).wait_send()
        for slot in goes_down if part < 2 else goes_down[:3] + goes_down[4:]:
            send_down(slot, part).wait_send()
        for slot in (0,) + goes_across + (() if part < 2 else (4,)):
            send_across(slot, part).wait_send()

    def finish():
        def one(step):
            source = lax.rem(me + step, N_CTX)
            row_copy(source, source, step).wait_recv()
            row_copy(source, source, step).wait_send()

        around(1, N_CTX, one)
        own_rows.wait()

    return finish


def layer(
    mixer,
    gate,
    dt,
    docs,
    taps,
    conv_bias,
    small,
    gain,
    attn_gain,
    w_out,
    residual,
    w_query,
    w_key,
    w_value,
    owners,
):
    rows, channels = mixer.shape
    heads = dt.shape[0]
    width = heads * P_SIZE
    share = residual.shape[1]
    half = rows // 2
    widths = (w_query.shape[1], w_key.shape[1], w_value.shape[1])
    total_width = sum(widths)
    shard_rows = w_query.shape[0] // 2
    group = widths[0] // HEAD_DIMENSION
    out_rows = (N_CTX, rows // N_CTX, widths[0])
    bf, f32 = jnp.bfloat16, jnp.float32
    state = (N_CTX, width // N_CTX, NS)
    piece = VMEM((half, share), bf)
    scratch = dict(
        mixer=VMEM(mixer.shape, bf),
        gate=VMEM(gate.shape, bf),
        dt=VMEM(dt.shape, f32),
        docs=VMEM(docs.shape, f32),
        docs_raw=VMEM(docs.shape, jnp.int32),
        taps=VMEM(taps.shape, f32),
        conv_bias=VMEM(conv_bias.shape, f32),
        dt_bias=VMEM((1, heads), f32),
        a_log=VMEM((1, heads), f32),
        d_skip=VMEM((1, heads), f32),
        gain=VMEM(gain.shape, f32),
        attn_gain=VMEM(attn_gain.shape, f32),
        residual=VMEM(residual.shape, bf),
        owners=VMEM(owners.shape, jnp.int32),
        shard=VMEM((shard_rows, total_width), bf),
        w_tiles=VMEM((N_T, w_out.shape[0], share), bf),
        load_sem=DMA((16,)),
        tile_sem=DMA((N_T,)),
        out_sem=DMA((2,)),
        extended=VMEM((rows + 8, channels), f32),
        docs_ext=VMEM((rows + 8, NS), f32),
        halo=VMEM((16, channels), bf),
        halo_send=DMA((2,)),
        halo_recv=DMA((2,)),
        conv=VMEM((rows, channels), bf),
        side=VMEM((N_CTX, 1, NS), f32),
        side_all=VMEM((N_CTX, 1, NS), f32),
        docs_all=VMEM((N_CTX,) + docs.shape, f32),
        docs_send=DMA((N_CTX,)),
        docs_recv=DMA((N_CTX,)),
        pieces=VMEM(state, bf),
        recv=VMEM(state, bf),
        scanned=VMEM(state, bf),
        incoming=VMEM(state, bf),
        base=VMEM((rows, width), f32),
        swish=VMEM((rows, width), f32),
        normed=VMEM((rows, width), bf),
        shards=VMEM((N_Z, shard_rows, total_width), bf),
        send1=DMA((N_CTX,)),
        recv1=DMA((N_CTX,)),
        send2=DMA((N_CTX,)),
        recv2=DMA((N_CTX,)),
        send3=DMA((N_CTX,)),
        recv3=DMA((N_CTX,)),
        up_send=DMA((4,)),
        up_recv=DMA((4,)),
        down_send=DMA((4,)),
        down_recv=DMA((4,)),
        relay_a=piece,
        relay_b=piece,
        accum_a=piece,
        accum_b=piece,
        direct_a=piece,
        direct_b=piece,
        stage=VMEM((6, half, share), bf),
        hold_a=VMEM((half, share), f32),
        hold_b=VMEM((half, share), f32),
        full=VMEM((N_T, 2, half, share), bf),
        gathered=VMEM((N_CTX, 2, shard_rows, total_width), bf),
        cosine=VMEM((rows, HEAD_DIMENSION), f32),
        sine=VMEM((rows, HEAD_DIMENSION), f32),
        starts=VMEM((1, group * rows), f32),
        rs_send=DMA((6,)),
        rs_recv=DMA((6,)),
        ag_send=DMA((6,)),
        ag_recv=DMA((6,)),
        cross_send=DMA((2, N_Z)),
        cross_recv=DMA((2, N_Z)),
        y_send=DMA((4,)),
        y_recv=DMA((4,)),
        core_send=DMA((4,)),
        core_recv=DMA((4,)),
        block=VMEM((2, N_T, half, share), bf),
        queries=VMEM((HEAD_DIMENSION, group * rows), bf),
        window=VMEM((WINDOW, 4, half, HEAD_DIMENSION), bf),
        outgoing=VMEM(out_rows, bf),
        best=VMEM((1, group * rows), f32),
        denom=VMEM((1, group * rows), f32),
        accum=VMEM((HEAD_DIMENSION, group * rows), f32),
        win_up_send=DMA((WINDOW, 4)),
        win_down_send=DMA((WINDOW, 4)),
        win_across_send=DMA((WINDOW, 4)),
        win_recv_sem=DMA((WINDOW, 4)),
        out_send=DMA((N_CTX,)),
        out_recv=DMA((N_CTX,)),
    )
    names = [
        "mixer_in",
        "gate_in",
        "dt_in",
        "docs_in",
        "taps_in",
        "conv_bias_in",
        "dt_bias_in",
        "a_log_in",
        "d_skip_in",
        "gain_in",
        "attn_gain_in",
        "w_out",
        "residual_in",
        "w_query",
        "w_key",
        "w_value",
        "owners_in",
        "hidden_ref",
        "out_ref",
    ] + list(scratch)

    def kernel(*refs):
        r = SimpleNamespace(**dict(zip(names, refs)))
        me = lax.axis_index("context")
        here = lax.axis_index("tensor")
        core = lax.axis_index("dp")
        barrier = pltpu.get_barrier_semaphore()

        def signal(peer):
            pl.semaphore_signal(barrier, inc=1, device_id=peer, device_id_type=MESH)

        around(1, N_CTX, lambda step: signal(context_peer(lax.rem(me + step, N_CTX))))
        signal(tensor_peer(lax.rem(here + 1, N_T)))
        signal(tensor_peer(lax.rem(here + 3, N_T)))
        signal({"dp": 1 - core})

        def load(src, dst, number):
            copy = pltpu.make_async_copy(src, dst, r.load_sem.at[number])
            copy.start()
            return copy

        r.load_docs = load(r.docs_in, r.docs_raw, 0)
        r.load_taps = load(r.taps_in, r.taps, 1)
        r.load_conv_bias = load(r.conv_bias_in, r.conv_bias, 10)
        r.load_small = [
            load(r.dt_bias_in, r.dt_bias, 11),
            load(r.a_log_in, r.a_log, 12),
            load(r.d_skip_in, r.d_skip, 13),
        ]
        r.load_mixer = load(r.mixer_in, r.mixer, 2)
        r.load_dt = load(r.dt_in, r.dt, 3)
        half_rows = pl.ds(core * shard_rows, shard_rows)
        r.load_shard = []
        begin = 0
        for number, (source, count) in enumerate(zip((r.w_query, r.w_key, r.w_value), widths)):
            r.load_shard.append(
                load(source.at[half_rows], r.shard.at[:, pl.ds(begin, count)], 4 + number)
            )
            begin += count
        r.load_gate = load(r.gate_in, r.gate, 7)
        r.load_gain = load(r.gain_in, r.gain, 14)
        r.load_attn_gain = load(r.attn_gain_in, r.attn_gain, 15)
        r.load_residual = load(r.residual_in, r.residual, 8)
        load_owners = load(r.owners_in, r.owners, 9)
        r.load_tiles = []
        for number, owner in enumerate((here + 2, here + 1, here + 3, here)):
            column = pl.multiple_of(lax.rem(owner, N_T) * share, share)
            copy = pltpu.make_async_copy(
                r.w_out.at[:, pl.ds(column, share)], r.w_tiles.at[number], r.tile_sem.at[number]
            )
            copy.start()
            r.load_tiles.append(copy)

        finish_mix, shards_arrive = mix_phase(r, me, core)
        finish_project, make_queries = project_phase(r, me, core, shards_arrive)
        load_owners.wait()
        finish_attend = attend_phase(r, me, make_queries)
        finish_mix()
        finish_project()
        finish_attend()

    anywhere = pl.BlockSpec(memory_space=pl.ANY)
    return pl.pallas_call(
        kernel,
        out_shape=(
            jax.ShapeDtypeStruct((2, half, share), bf),
            jax.ShapeDtypeStruct(out_rows, bf),
        ),
        in_specs=[anywhere] * 17,
        out_specs=(anywhere, anywhere),
        scratch_shapes=list(scratch.values()),
        compiler_params=pltpu.CompilerParams(
            collective_id=0, has_side_effects=True, vmem_limit_bytes=60 * 1024 * 1024
        ),
        name="layer",
    )(
        mixer,
        gate,
        dt,
        docs,
        taps,
        conv_bias,
        *small,
        gain,
        attn_gain,
        w_out,
        residual,
        w_query,
        w_key,
        w_value,
        owners,
    )


def per_device(
    mixer_input,
    gate_z,
    dt_raw,
    dt_bias,
    a_log,
    d_skip,
    conv_weight,
    conv_bias,
    norm_gain,
    w_out,
    residual,
    attn_gain,
    w_query,
    w_key,
    value_weight,
    doc_ids,
    owners,
):
    row_count, channels = mixer_input.shape
    share = residual.shape[1]

    hidden_out, attended = layer(
        mixer_input,
        gate_z,
        dt_raw.T,
        doc_ids.reshape(row_count // NS, NS),
        conv_weight,
        conv_bias.reshape(channels // NS, NS),
        (dt_bias[None, :], a_log[None, :], d_skip[None, :]),
        norm_gain[None, :],
        attn_gain.reshape(-1, NS),
        w_out,
        residual,
        w_query,
        w_key,
        value_weight,
        owners,
    )
    return (
        hidden_out.reshape(row_count, share),
        attended.reshape(row_count, w_query.shape[1]),
    )


def solution(mesh):
    in_specs = (
        P(("dp", "context"), "tensor"),
        P(("dp", "context"), "tensor"),
        P(("dp", "context"), "tensor"),
        P("tensor"),
        P("tensor"),
        P("tensor"),
        P(None, "tensor"),
        P("tensor"),
        P("tensor"),
        P("tensor", None),
        P(("dp", "context"), "tensor"),
        P(),
        P("context", "tensor"),
        P("context", "tensor"),
        P("context", "tensor"),
        P(("dp", "context")),
        P(("dp", "context"), None),
    )
    out_specs = (P(("dp", "context"), "tensor"), P(("dp", "context"), "tensor"))
    return jax.shard_map(
        per_device, mesh=mesh, in_specs=in_specs, out_specs=out_specs, check_vma=False
    )
```
